512 devices in a mesh: prow: 16 (over y, z_hi), pcol: 32 (over x, z_lo, core).
Axes of the slice: x: 4, y: 4, z: 16 (z_hi: 4, z_lo: 4; z = z_hi * 4 + z_lo), core: 2. Of those that a mesh axis runs over, the one named last changes fastest.
Arguments:
- window: float32 [16384, 16384], P('prow', 'pcol'), may hold values from -6 to 6
- panel: float32 [16384, 256], P(('prow', 'pcol')), may hold values from -0.046875 to 0.046875
- factor: float32 [256, 256], replicated, may hold values from -1 to 1
- col_check: float32 [16384], P('pcol'), may hold values from -6 to 6
- row_check: float32 [16384], P('prow'), may hold values from -6 to 6
Outputs:
- new_window: float32 [16384, 16384], P('prow', 'pcol')
- new_col: float32 [16384], P('pcol')
- new_row: float32 [16384], P('prow')
The draws below stay inside these ranges and needn't reach their ends.
All inputs are finite; a program needn't handle non-finite values.
Results may differ from the reference program's by a relative error of at most 0.00005.
Values sent between devices are 32-bit elements; how exact they have to be, the bound alone decides.
No kernel may reach another device: no remote copies, remote signals or barrier semaphores. Data moves between devices by JAX's collectives and lax.ppermute only.
A program may use at most 64 MiB of HBM per device.

```python
import math
import jax
import jax.numpy as jnp
from jax import lax

N = 16384
K = 256


def level_of(stream_key, dims, shards, low, top_value):
    loudness, own = 1.0, jax.random.fold_in(stream_key, 6)
    for position, parts in shards:
        steps = jnp.exp(jax.random.uniform(jax.random.fold_in(own, position), (parts,), jnp.float32, low / len(shards), top_value / len(shards)))
        loudness = loudness * jnp.repeat(steps, dims[position] // parts).reshape([-1 if axis == position else 1 for axis in range(len(dims))])
    return loudness


def centred(stream_key, dims, scale, bound, split=(), kind=jnp.bfloat16):
    result = jax.random.normal(stream_key, dims, jnp.float32) * scale
    if len(split) > 0:
        result = level_of(stream_key, dims, split, -0.22, 0.18) * result
    return jnp.clip(result, min=-bound, max=bound).astype(kind)


def setup_inputs(seed: int = 0) -> dict:
    keys = jax.random.split(jax.random.key(seed), 6)
    window = centred(keys[0], (N, N), 1.0, 6.0, ((0, 16), (1, 32)), jnp.float32)
    panel = centred(keys[1], (N, K), N ** -0.5, 0.046875, ((0, 512),), jnp.float32)
    factor = centred(keys[2], (K, K), (1.0 / K ** 0.5), 1.0, (), jnp.float32)
    col_check = centred(keys[3], (N,), 1.0, 6.0, ((0, 32),), jnp.float32)
    row_check = centred(keys[4], (N,), 1.0, 6.0, ((0, 16),), jnp.float32)
    return {"window": window, "panel": panel, "factor": factor, "col_check": col_check, "row_check": row_check}


def unit_lower(values, row_start):
    rows = row_start + jnp.arange(values.shape[0], dtype=jnp.int32)[:, None]
    cols = jnp.arange(values.shape[1], dtype=jnp.int32)[None, :]
    ones = jnp.where(rows == cols, jnp.ones_like(values), jnp.zeros_like(values))
    return jnp.where(rows > cols, values, ones)

def reference(window, panel, factor, col_check, row_check):
    high = lax.Precision.HIGHEST
    refl = unit_lower(panel, 0)
    upper = jnp.triu(factor)
    x_prod = jnp.dot(window, refl, precision=high)
    y_prod = jnp.dot(x_prod, upper, precision=high)
    w_prod = jnp.dot(refl.T, window, precision=high)
    z_prod = jnp.dot(refl.T, y_prod, precision=high)
    m_prod = jnp.dot(upper.T, w_prod - jnp.dot(z_prod, refl.T, precision=high), precision=high)
    left = jnp.concatenate([y_prod, refl], axis=1)
    right = jnp.concatenate([refl.T, m_prod], axis=0)
    new_window = window - jnp.dot(left, right, precision=high)
    scaled = lax.optimization_barrier(jnp.sum(refl, axis=0)) / math.sqrt(N)
    col_proj = jnp.dot(col_check, refl, precision=high)
    row_proj = jnp.dot(row_check, refl, precision=high)
    new_col = col_check - jnp.dot(refl, jnp.dot(col_proj, upper, precision=high), precision=high) - jnp.dot(scaled, m_prod, precision=high)
    inner = row_proj - jnp.dot(z_prod, scaled, precision=high)
    new_row = row_check - jnp.dot(y_prod, scaled, precision=high) - jnp.dot(refl, jnp.dot(inner, upper, precision=high), precision=high)
    return (new_window, new_col, new_row)
```

```python
import math

import jax
import jax.numpy as jnp
from jax import lax
from jax.sharding import Mesh, PartitionSpec as P

N = 16384
AXES = ("y", "zh", "x", "zl", "core")
SIZES = (4, 4, 4, 4, 2)
PREC = lax.Precision.HIGHEST


def dot(left, right, dims=((1,), (0,))):
    return lax.dot_general(left, right, (dims, ((), ())), precision=PREC)


def unit_lower(values, row_start):
    rows = row_start + lax.broadcasted_iota(jnp.int32, values.shape, 0)
    cols = lax.broadcasted_iota(jnp.int32, values.shape, 1)
    return jnp.where(rows > cols, values, jnp.where(rows == cols, 1.0, 0.0))


def exchange(parts, axis):
    return lax.all_to_all(parts, axis, 0, 0)


def gather(block, axis, size):
    parts = exchange(jnp.broadcast_to(block[None], (size,) + block.shape), axis)
    return parts.reshape((size * block.shape[0],) + block.shape[1:])


def reduce_scatter(block, axis, size):
    rows = block.shape[0] // size
    return jnp.sum(exchange(block.reshape(size, rows, block.shape[1]), axis), axis=0)


def reduce_both(block, small, axis, size):
    rows = block.shape[0] // size
    cut = block.reshape(size, rows, block.shape[1])
    both = jnp.concatenate([cut, jnp.broadcast_to(small[None], (size,) + small.shape)], axis=1)
    total = jnp.sum(exchange(both, axis), axis=0)
    return total[:rows], total[rows:]


def transposition():
    pairs = []
    for y in range(4):
        for zh in range(4):
            for x in range(4):
                for zl in range(4):
                    for core in range(2):
                        src = (((y * 4 + zh) * 4 + x) * 4 + zl) * 2 + core
                        dst = (((x * 4 + zl) * 4 + y) * 4 + zh) * 2 + core
                        pairs.append((src, dst))
    return pairs


def on_device(window, panel, factor, col_check, row_check):
    y, zh, core = lax.axis_index("y"), lax.axis_index("zh"), lax.axis_index("core")
    prow = y * 4 + zh
    kdim = panel.shape[1]
    shard = panel.shape[0]
    n_rows, n_cols = window.shape
    upper = jnp.triu(factor)

    mine = gather(panel, ("x", "zl"), 16)
    other = lax.ppermute(mine, "core", [(0, 1), (1, 0)])
    mine, other = (v.reshape(16, 1, shard, kdim) for v in (mine, other))
    first = jnp.where(core == 0, mine, other)
    second = jnp.where(core == 0, other, mine)
    v_rows = jnp.concatenate([first, second], axis=1).reshape(n_rows, kdim)
    v_rows = unit_lower(v_rows, prow * n_rows)

    half = lax.dynamic_slice_in_dim(v_rows, core * n_cols, n_cols, 0)
    v_cols = lax.ppermute(half, AXES, transposition())

    w_part = dot(v_rows, window, ((0,), (0,)))
    w_part = reduce_scatter(w_part, "y", 4)
    w_slice = reduce_scatter(w_part, "zh", 4)
    row_part = dot(row_check[None], v_rows)

    x_part = dot(window, v_cols)
    p_part = dot(w_slice, v_cols)
    col_part = dot(col_check[None], v_cols)
    sum_part = jnp.sum(v_cols, axis=0, keepdims=True)
    small = jnp.concatenate([p_part, col_part, sum_part, jnp.zeros((6, kdim), jnp.float32)], axis=0)
    x_part, small = reduce_both(x_part, small, "core", 2)
    x_part, small = reduce_both(x_part, small, "x", 4)
    x_slice, small = reduce_both(x_part, small, "zl", 4)
    k_rows = w_slice.shape[0]
    p_slice, col_proj, sums = small[:k_rows], small[k_rows], small[k_rows + 1]
    scaled = sums / math.sqrt(N)

    z_slice = dot(p_slice, upper)
    g_slice = w_slice - dot(z_slice, v_cols, ((1,), (1,)))
    z_scaled = dot(scaled[None], z_slice, ((1,), (1,)))
    lanes = 128
    extra = jnp.concatenate(
        [
            row_part.reshape(kdim // lanes, lanes),
            jnp.pad(z_scaled, ((0, 0), (0, lanes - k_rows))),
            jnp.zeros((k_rows - kdim // lanes - 1, lanes), jnp.float32),
        ],
        axis=0,
    )
    g_all = gather(jnp.concatenate([g_slice, extra], axis=1), "zh", 4)
    g_all = gather(g_all, "y", 4)
    g_full = g_all[:, :n_cols]
    extras = g_all[:, n_cols:].reshape(16, k_rows, lanes)
    row_proj = jnp.sum(extras[:, : kdim // lanes], axis=0).reshape(kdim)
    inner = row_proj - extras[:, kdim // lanes, :k_rows].reshape(kdim)

    x_rows = gather(x_slice, "zl", 4)
    x_rows = gather(x_rows, "x", 4)
    x_rows = gather(x_rows, "core", 2)

    y_rows = dot(x_rows, upper)
    m_trans = dot(g_full, upper, ((0,), (0,)))
    left = jnp.concatenate([y_rows, v_rows], axis=1)
    right = jnp.concatenate([v_cols, m_trans], axis=1)
    new_window = window - dot(left, right, ((1,), (1,)))
    col_vec = jnp.concatenate([dot(col_proj[None], upper)[0], scaled])
    row_vec = jnp.concatenate([scaled, dot(inner[None], upper)[0]])
    new_col = col_check - dot(col_vec[None], right, ((1,), (1,)))[0]
    new_row = row_check - dot(row_vec[None], left, ((1,), (1,)))[0]
    return (new_window, new_col, new_row)


def solution(mesh):
    fine = Mesh(mesh.devices.reshape(SIZES), AXES)
    rows, cols = ("y", "zh"), ("x", "zl", "core")
    placed = (P(rows, cols), P(AXES, None), P(), P(cols), P(rows))
    return jax.shard_map(
        on_device,
        mesh=fine,
        in_specs=placed,
        out_specs=(P(rows, cols), P(cols), P(rows)),
        check_vma=False,
    )
```

```python
import math

import jax
import jax.numpy as jnp
from jax import lax
from jax.experimental import pallas as pl
from jax.experimental.pallas import tpu as pltpu
from jax.sharding import Mesh, PartitionSpec as P


N = 16384
AXES = ("y", "zh", "x", "zl", "core")
SIZES = (4, 4, 4, 4, 2)
PREC = lax.Precision.HIGH


def dot(left, right, dims=((1,), (0,))):
    return lax.dot_general(left, right, (dims, ((), ())), precision=PREC)


def unit_lower(values, row_start):
    rows = row_start + lax.broadcasted_iota(jnp.int32, values.shape, 0)
    cols = lax.broadcasted_iota(jnp.int32, values.shape, 1)
    return jnp.where(rows > cols, values, jnp.where(rows == cols, 1.0, 0.0))


def exchange(parts, axis):
    return lax.all_to_all(parts, axis, 0, 0)


def gather(block, axis, size):
    parts = exchange(jnp.broadcast_to(block[None], (size,) + block.shape), axis)
    return parts.reshape((size * block.shape[0],) + block.shape[1:])


def reduce_scatter(block, axis, size):
    rows = block.shape[0] // size
    return jnp.sum(exchange(block.reshape(size, rows, block.shape[1]), axis), axis=0)


def reduce_both(block, small, axis, size):
    rows = block.shape[0] // size
    cut = block.reshape(size, rows, block.shape[1])
    both = jnp.concatenate([cut, jnp.broadcast_to(small[None], (size,) + small.shape)], axis=1)
    total = jnp.sum(exchange(both, axis), axis=0)
    return total[:rows], total[rows:]


def swap(block, axis, size, bit):
    return lax.ppermute(block, axis, [(i, i ^ bit) for i in range(size)])


def ordered(mine, other, bit, axis):
    own = jnp.expand_dims(mine, axis)
    far = jnp.expand_dims(other, axis)
    shape = own.shape[:axis] + (2,) + own.shape[axis + 1 :]
    out = jnp.zeros(shape, mine.dtype)
    out = lax.dynamic_update_slice(out, own, [bit if i == axis else 0 for i in range(len(shape))])
    return lax.dynamic_update_slice(out, far, [1 - bit if i == axis else 0 for i in range(len(shape))])


def double(block, axis, size, bit):
    index = lax.axis_index(axis)
    other = swap(block, axis, size, bit)
    out = ordered(block, other, (index & bit) // bit, 0)
    return out.reshape((2 * block.shape[0],) + block.shape[1:])


def transposition():
    pairs = []
    for y in range(4):
        for zh in range(4):
            for x in range(4):
                for zl in range(4):
                    for core in range(2):
                        src = (((y * 4 + zh) * 4 + x) * 4 + zl) * 2 + core
                        new_y = x % 2 * 2 + core
                        dst = (((new_y * 4 + zl) * 4 + y) * 4 + zh) * 2 + x // 2
                        pairs.append((src, dst))
    return pairs


def split(value):
    high = value.astype(jnp.bfloat16)
    return high, (value - high.astype(jnp.float32)).astype(jnp.bfloat16)


def mm(left, right, dims):
    def one(a, b):
        return lax.dot_general(a, b, (dims, ((), ())), preferred_element_type=jnp.float32)

    (lh, ll), (rh, rl) = left, right
    return one(lh, rh) + (one(lh, rl) + one(ll, rh))


NN = ((1,), (0,))
NT = ((1,), (1,))
TN = ((0,), (0,))
STEPS = 4


VMEM = pl.BlockSpec(memory_space=pltpu.VMEM)
SMEM = pl.BlockSpec(memory_space=pltpu.SMEM)
HBM = pl.BlockSpec(memory_space=pltpu.HBM)


def f32(*shape):
    return jax.ShapeDtypeStruct(shape, jnp.float32)


def block_copy(src, dst, sems, step):
    rows = src.shape[0] // STEPS
    part = pl.ds(step * rows, rows)
    return pltpu.make_async_copy(src.at[part], dst.at[part], sems.at[step])


def interleaved(lead, own, far):
    groups, shard, kdim = own.shape
    first = jnp.where(lead > 0.5, own, far)
    second = jnp.where(lead > 0.5, far, own)
    return jnp.concatenate([first, second], axis=1).reshape(2 * groups * shard, kdim)


def rows_kernel(where_ref, mine_ref, other_ref, check_ref, window_ref, v_ref, w_ref, u_ref, buf, sems):
    for step in range(STEPS):
        block_copy(window_ref, buf, sems, step).start()
    lead = jnp.where(where_ref[0] == 0, 1.0, 0.0)
    groups, rows = mine_ref.shape[0] // STEPS, v_ref.shape[0] // STEPS
    for step in range(STEPS):
        mine, other = (ref[step * groups : (step + 1) * groups] for ref in (mine_ref, other_ref))
        block = unit_lower(interleaved(lead, mine, other), where_ref[1] + step * rows)
        part = slice(step * rows, (step + 1) * rows)
        v_ref[part] = block
        parts = split(block)
        block_copy(window_ref, buf, sems, step).wait()
        w_part = mm(parts, split(buf[part]), TN)
        u_part = mm(split(jnp.broadcast_to(check_ref[:, part], (8, rows))), parts, NN)[:1]
        if step == 0:
            w_ref[...] = w_part
            u_ref[...] = u_part
        else:
            w_ref[...] += w_part
            u_ref[...] += u_part


def rows_call(where, mine, other, window, check):
    n_rows, n_cols = window.shape
    kdim = mine.shape[2]
    return pl.pallas_call(
        rows_kernel,
        in_specs=[SMEM, VMEM, VMEM, VMEM, HBM],
        out_specs=[VMEM] * 3,
        out_shape=[f32(n_rows, kdim), f32(kdim, n_cols), f32(1, kdim)],
        scratch_shapes=[pltpu.VMEM((n_rows, n_cols), jnp.float32), pltpu.SemaphoreType.DMA((STEPS,))],
        name="rows",
    )(where, mine, other, check.reshape(1, n_rows), window)


def cols_kernel(where_ref, own_ref, far_ref, check_ref, window_ref, v_ref, keep_ref, send_ref, tail_ref, buf, sems):
    for step in range(STEPS):
        block_copy(window_ref, buf, sems, step).start()
    lead = jnp.where(where_ref[0] == 0, 1.0, 0.0)
    block = unit_lower(interleaved(lead, own_ref[...], far_ref[...]), where_ref[1])
    v_ref[...] = block
    parts = split(block)
    line = lax.broadcasted_iota(jnp.int32, (8, check_ref.shape[1]), 0)
    tail = jnp.where(line == 0, check_ref[...], jnp.where(line == 1, 1.0, 0.0))
    tail_ref[...] = mm(split(tail), parts, NN)
    half, rows = STEPS // 2, window_ref.shape[0] // STEPS
    for step in range(STEPS):
        block_copy(window_ref, buf, sems, step).wait()
        x = mm(split(buf[step * rows : (step + 1) * rows]), parts, NN)
        part = slice(step % half * rows, (step % half + 1) * rows)

        @pl.when(where_ref[2] == step // half)
        def _():
            keep_ref[part] = x

        @pl.when(where_ref[2] != step // half)
        def _():
            send_ref[part] = x


def cols_call(where, own, far, check, window):
    n_rows, n_cols = window.shape
    kdim = own.shape[2]
    return pl.pallas_call(
        cols_kernel,
        in_specs=[SMEM, VMEM, VMEM, VMEM, HBM],
        out_specs=[VMEM] * 4,
        out_shape=[f32(n_cols, kdim), f32(n_rows // 2, kdim), f32(n_rows // 2, kdim), f32(8, kdim)],
        scratch_shapes=[pltpu.VMEM((n_rows, n_cols), jnp.float32), pltpu.SemaphoreType.DMA((STEPS,))],
        name="cols",
    )(where, own, far, check.reshape(1, n_cols), window)


def left_kernel(where_ref, own_ref, far_ref, c_ref, u_ref, vec_ref, row_ref, col_ref, window_ref, nrow_ref, ncol_ref, out_ref, buf, sems, done):
    for step in range(STEPS):
        block_copy(window_ref, buf, sems, step).start()
    c_parts = split(c_ref[...])
    vec = vec_ref[...]
    turned = mm(split(vec), split(u_ref[...]), NN)
    ncol_ref[...] = col_ref[...] - mm(split(turned), c_parts, NT)[1:2]
    vec_parts = split(vec)
    half, rows = STEPS // 2, window_ref.shape[0] // STEPS
    lead = jnp.where(where_ref[0] == 0, 1.0, 0.0)
    for step in range(STEPS):
        piece = slice(step % half * rows, (step % half + 1) * rows)
        mine = lead if step < half else 1.0 - lead
        y_parts = split(jnp.where(mine > 0.5, own_ref[piece], far_ref[piece]))
        part = slice(step * rows, (step + 1) * rows)
        out = mm(y_parts, c_parts, NT)
        block_copy(window_ref, buf, sems, step).wait()
        buf[part] = buf[part] - out
        block_copy(buf, out_ref, done, step).start()
        nrow_ref[:, part] = row_ref[:, part] - mm(vec_parts, y_parts, NT)[:1]
    for step in range(STEPS):
        block_copy(buf, out_ref, done, step).wait()


def left_call(where, own, far, v_cols, upper, vectors, row_check, col_check, window):
    n_rows, n_cols = window.shape
    return pl.pallas_call(
        left_kernel,
        in_specs=[SMEM] + [VMEM] * 7 + [HBM],
        out_specs=[VMEM, VMEM, HBM],
        out_shape=[f32(1, n_rows), f32(1, n_cols), f32(n_rows, n_cols)],
        scratch_shapes=[
            pltpu.VMEM((n_rows, n_cols), jnp.float32),
            pltpu.SemaphoreType.DMA((STEPS,)),
            pltpu.SemaphoreType.DMA((STEPS,)),
        ],
        name="left",
    )(where, own, far, v_cols, upper, vectors, row_check.reshape(1, n_rows), col_check.reshape(1, n_cols), window)


def right_kernel(v_ref, g_ref, u_ref, vec_ref, row_ref, col_ref, window_ref, nrow_ref, ncol_ref, out_ref, buf, sems, done):
    for step in range(STEPS):
        block_copy(window_ref, buf, sems, step).start()
    n_cols = window_ref.shape[1]
    kdim = u_ref.shape[0]
    upper = split(u_ref[...])
    g_all = g_ref[...]
    m_parts = split(mm(upper, split(g_all[:, :n_cols]), TN))
    ncol_ref[...] = col_ref[...] - mm(split(vec_ref[...]), m_parts, NN)[:1]
    lanes = g_all.shape[1] - n_cols
    extra = jnp.sum(g_all[:, n_cols:].reshape(16, kdim // 16, lanes), axis=0)
    inner = jnp.concatenate([extra[i : i + 1] for i in range(kdim // lanes)], axis=1)
    inner = split(mm(split(jnp.broadcast_to(inner, (8, kdim))), upper, NN))
    rows = window_ref.shape[0] // STEPS
    for step in range(STEPS):
        part = slice(step * rows, (step + 1) * rows)
        v_parts = split(v_ref[part])
        out = mm(v_parts, m_parts, NN)
        block_copy(window_ref, buf, sems, step).wait()
        buf[part] = buf[part] - out
        block_copy(buf, out_ref, done, step).start()
        nrow_ref[:, part] = row_ref[:, part] - mm(inner, v_parts, NT)[:1]
    for step in range(STEPS):
        block_copy(buf, out_ref, done, step).wait()


def right_call(v_rows, g_all, upper, vectors, row_part, col_part, window):
    n_rows, n_cols = window.shape
    return pl.pallas_call(
        right_kernel,
        in_specs=[VMEM] * 6 + [HBM],
        out_specs=[VMEM, VMEM, HBM],
        out_shape=[f32(1, n_rows), f32(1, n_cols), f32(n_rows, n_cols)],
        scratch_shapes=[
            pltpu.VMEM((n_rows, n_cols), jnp.float32),
            pltpu.SemaphoreType.DMA((STEPS,)),
            pltpu.SemaphoreType.DMA((STEPS,)),
        ],
        name="right",
    )(v_rows, g_all, upper, vectors, row_part, col_part, window)


def on_device(window, panel, factor, col_check, row_check):
    y, zh, core = lax.axis_index("y"), lax.axis_index("zh"), lax.axis_index("core")
    x, zl = lax.axis_index("x"), lax.axis_index("zl")
    prow = y * 4 + zh
    pcol = (x * 4 + zl) * 2 + core
    kdim = panel.shape[1]
    shard = panel.shape[0]
    n_rows, n_cols = window.shape
    upper = jnp.triu(factor)

    mine = gather(panel, ("x", "zl"), 16)
    quarter = lax.dynamic_slice_in_dim(mine, x // 2 * (n_cols // 2), n_cols // 2, 0)
    moved = lax.ppermute(quarter, AXES, transposition())
    other = swap(mine, "core", 2, 1)
    v_rows, w_part, row_part = rows_call(
        jnp.stack([core, prow * n_rows]).astype(jnp.int32),
        mine.reshape(-1, shard, kdim),
        other.reshape(-1, shard, kdim),
        window,
        row_check,
    )
    w_part = reduce_scatter(w_part, "y", 4)
    near = swap(moved, "y", 4, 1)
    w_slice = reduce_scatter(w_part, "zh", 4)

    k_rows = w_slice.shape[0]
    v_cols, keep, send, tail = cols_call(
        jnp.stack([y % 2, pcol * n_cols, core]).astype(jnp.int32),
        moved.reshape(-1, shard, kdim),
        near.reshape(-1, shard, kdim),
        col_check,
        window,
    )
    x_part = keep + swap(send, "core", 2, 1)
    small = jnp.concatenate([dot(w_slice, v_cols), tail], axis=0)
    x_part, small = reduce_both(x_part, small, "x", 4)
    x_slice, small = reduce_both(x_part, small, "zl", 4)
    small = small + swap(small, "core", 2, 1)
    p_slice, col_proj, sums = small[:k_rows], small[k_rows], small[k_rows + 1]
    scaled = sums / math.sqrt(N)
    vectors = jnp.concatenate([scaled[None], col_proj[None], jnp.zeros((6, kdim), jnp.float32)], axis=0)

    y_rows = dot(x_slice, upper)
    y_rows = double(y_rows, "zl", 4, 1)
    y_rows = double(y_rows, "zl", 4, 2)
    y_rows = gather(y_rows, "x", 4)
    y_far = swap(y_rows, "core", 2, 1)

    z_slice = dot(p_slice, upper)
    g_slice = w_slice - dot(z_slice, v_cols, ((1,), (1,)))
    z_scaled = dot(scaled[None], z_slice, ((1,), (1,)))
    lanes = 128
    owner = lax.broadcasted_iota(jnp.int32, (1, kdim), 1) // k_rows
    partial = row_part - jnp.where(owner == prow, jnp.tile(z_scaled, (1, kdim // k_rows)), 0.0)
    extra = jnp.pad(partial.reshape(kdim // lanes, lanes), ((0, k_rows - kdim // lanes), (0, 0)))
    g_all = gather(jnp.concatenate([g_slice, extra], axis=1), "zh", 4)
    g_all = gather(g_all, "y", 4)

    new_row, new_col, partly = left_call(
        core[None].astype(jnp.int32), y_rows, y_far, v_cols, upper, vectors, row_check, col_check, window
    )
    new_row, new_col, new_window = right_call(v_rows, g_all, upper, vectors, new_row, new_col, partly)
    return new_window, new_col.reshape(n_cols), new_row.reshape(n_rows)


def solution(mesh):
    fine = Mesh(mesh.devices.reshape(SIZES), AXES)
    rows, cols = ("y", "zh"), ("x", "zl", "core")
    placed = (P(rows, cols), P(AXES, None), P(), P(cols), P(rows))
    return jax.shard_map(
        on_device,
        mesh=fine,
        in_specs=placed,
        out_specs=(P(rows, cols), P(cols), P(rows)),
        check_vma=False,
    )
```

```python
import math

import jax
import jax.numpy as jnp
from jax import lax
from jax.experimental import pallas as pl
from jax.experimental.pallas import tpu as pltpu
from jax.sharding import Mesh, PartitionSpec as P


N = 16384
AXES = ("y", "zh", "x", "zl", "core")
SIZES = (4, 4, 4, 4, 2)
PREC = lax.Precision.HIGH


def dot(left, right, dims=((1,), (0,))):
    return lax.dot_general(left, right, (dims, ((), ())), precision=PREC)


def unit_lower(values, row_start):
    rows = row_start + lax.broadcasted_iota(jnp.int32, values.shape, 0)
    cols = lax.broadcasted_iota(jnp.int32, values.shape, 1)
    return jnp.where(rows > cols, values, jnp.where(rows == cols, 1.0, 0.0))


def exchange(parts, axis):
    return lax.all_to_all(parts, axis, 0, 0)


def gather(block, axis, size):
    parts = exchange(jnp.broadcast_to(block[None], (size,) + block.shape), axis)
    return parts.reshape((size * block.shape[0],) + block.shape[1:])


def reduce_scatter(block, axis, size):
    rows = block.shape[0] // size
    return jnp.sum(exchange(block.reshape(size, rows, block.shape[1]), axis), axis=0)


def reduce_both(block, small, axis, size):
    rows = block.shape[0] // size
    cut = block.reshape(size, rows, block.shape[1])
    both = jnp.concatenate([cut, jnp.broadcast_to(small[None], (size,) + small.shape)], axis=1)
    total = jnp.sum(exchange(both, axis), axis=0)
    return total[:rows], total[rows:]


def swap(block, axis, size, bit):
    return lax.ppermute(block, axis, [(i, i ^ bit) for i in range(size)])


def transposition():
    pairs = []
    for y in range(4):
        for zh in range(4):
            for x in range(4):
                for zl in range(4):
                    for core in range(2):
                        src = (((y * 4 + zh) * 4 + x) * 4 + zl) * 2 + core
                        new_y = x % 2 * 2 + core
                        dst = (((new_y * 4 + zl) * 4 + y) * 4 + zh) * 2 + x // 2
                        pairs.append((src, dst))
    return pairs


def split(value):
    high = value.astype(jnp.bfloat16)
    return high, (value - high.astype(jnp.float32)).astype(jnp.bfloat16)


def mm(left, right, dims):
    def one(a, b):
        return lax.dot_general(a, b, (dims, ((), ())), preferred_element_type=jnp.float32)

    (lh, ll), (rh, rl) = left, right
    return one(lh, rh) + (one(lh, rl) + one(ll, rh))


NN = ((1,), (0,))
NT = ((1,), (1,))
TN = ((0,), (0,))
STEPS = 4


VMEM = pl.BlockSpec(memory_space=pltpu.VMEM)
SMEM = pl.BlockSpec(memory_space=pltpu.SMEM)
HBM = pl.BlockSpec(memory_space=pltpu.HBM)


def f32(*shape):
    return pltpu.VMEM(shape, jnp.float32)


def vmem(value):
    return pltpu.with_memory_space_constraint(value, pltpu.VMEM)


def block_copy(src, dst, sems, step):
    rows = src.shape[0] // STEPS
    part = pl.ds(step * rows, rows)
    return pltpu.make_async_copy(src.at[part], dst.at[part], sems.at[step])


def interleaved(lead, own, far):
    groups, shard, kdim = own.shape
    first = jnp.where(lead > 0.5, own, far)
    second = jnp.where(lead > 0.5, far, own)
    return jnp.concatenate([first, second], axis=1).reshape(2 * groups * shard, kdim)


def rows_kernel(where_ref, mine_ref, other_ref, check_ref, window_ref, v_ref, w_ref, u_ref, buf, sems):
    for step in range(STEPS):
        block_copy(window_ref, buf, sems, step).start()
    lead = jnp.where(where_ref[0] == 0, 1.0, 0.0)
    groups, rows = mine_ref.shape[0] // STEPS, v_ref.shape[0] // STEPS
    for step in range(STEPS):
        mine, other = (ref[step * groups : (step + 1) * groups] for ref in (mine_ref, other_ref))
        block = unit_lower(interleaved(lead, mine, other), where_ref[1] + step * rows)
        part = slice(step * rows, (step + 1) * rows)
        v_ref[part] = block
        parts = split(block)
        block_copy(window_ref, buf, sems, step).wait()
        w_part = mm(parts, split(buf[part]), TN)
        u_part = mm(split(jnp.broadcast_to(check_ref[:, part], (8, rows))), parts, NN)[:1]
        if step == 0:
            w_ref[...] = w_part
            u_ref[...] = u_part
        else:
            w_ref[...] += w_part
            u_ref[...] += u_part


def rows_call(where, mine, other, window, check):
    n_rows, n_cols = window.shape
    kdim = mine.shape[2]
    return pl.pallas_call(
        rows_kernel,
        in_specs=[SMEM, VMEM, VMEM, VMEM, HBM],
        out_specs=[VMEM] * 3,
        out_shape=[f32(n_rows, kdim), f32(kdim, n_cols), f32(1, kdim)],
        scratch_shapes=[pltpu.VMEM((n_rows, n_cols), jnp.float32), pltpu.SemaphoreType.DMA((STEPS,))],
        name="rows",
    )(where, vmem(mine), vmem(other), check.reshape(1, n_rows), window)


def cols_kernel(where_ref, own_ref, far_ref, check_ref, window_ref, v_ref, keep_ref, send_ref, tail_ref, buf, sems):
    for step in range(STEPS):
        block_copy(window_ref, buf, sems, step).start()
    lead = jnp.where(where_ref[0] == 0, 1.0, 0.0)
    block = unit_lower(interleaved(lead, own_ref[...], far_ref[...]), where_ref[1])
    v_ref[...] = block
    parts = split(block)
    line = lax.broadcasted_iota(jnp.int32, (8, check_ref.shape[1]), 0)
    tail = jnp.where(line == 0, check_ref[...], jnp.where(line == 1, 1.0, 0.0))
    tail_ref[...] = mm(split(tail), parts, NN)
    half, rows = STEPS // 2, window_ref.shape[0] // STEPS
    for step in range(STEPS):
        block_copy(window_ref, buf, sems, step).wait()
        x = mm(split(buf[step * rows : (step + 1) * rows]), parts, NN)
        part = slice(step % half * rows, (step % half + 1) * rows)

        @pl.when(where_ref[2] == step // half)
        def _():
            keep_ref[part] = x

        @pl.when(where_ref[2] != step // half)
        def _():
            send_ref[part] = x


def cols_call(where, own, far, check, window):
    n_rows, n_cols = window.shape
    kdim = own.shape[2]
    return pl.pallas_call(
        cols_kernel,
        in_specs=[SMEM, VMEM, VMEM, VMEM, HBM],
        out_specs=[VMEM] * 4,
        out_shape=[f32(n_cols, kdim), f32(n_rows // 2, kdim), f32(n_rows // 2, kdim), f32(8, kdim)],
        scratch_shapes=[pltpu.VMEM((n_rows, n_cols), jnp.float32), pltpu.SemaphoreType.DMA((STEPS,))],
        name="cols",
    )(where, vmem(own), vmem(far), check.reshape(1, n_cols), window)


def left_kernel(where_ref, own_ref, far_ref, c_ref, u_ref, vec_ref, row_ref, col_ref, window_ref, nrow_ref, ncol_ref, out_ref, buf, sems, done):
    for step in range(STEPS):
        block_copy(window_ref, buf, sems, step).start()
    c_parts = split(c_ref[...])
    vec = vec_ref[...]
    turned = mm(split(vec), split(u_ref[...]), NN)
    ncol_ref[...] = col_ref[...] - mm(split(turned), c_parts, NT)[1:2]
    vec_parts = split(vec)
    half, rows = STEPS // 2, window_ref.shape[0] // STEPS
    lead = jnp.where(where_ref[0] == 0, 1.0, 0.0)
    for step in range(STEPS):
        piece = slice(step % half * rows, (step % half + 1) * rows)
        mine = lead if step < half else 1.0 - lead
        y_parts = split(jnp.where(mine > 0.5, own_ref[piece], far_ref[piece]))
        part = slice(step * rows, (step + 1) * rows)
        out = mm(y_parts, c_parts, NT)
        block_copy(window_ref, buf, sems, step).wait()
        buf[part] = buf[part] - out
        block_copy(buf, out_ref, done, step).start()
        nrow_ref[:, part] = row_ref[:, part] - mm(vec_parts, y_parts, NT)[:1]
    for step in range(STEPS):
        block_copy(buf, out_ref, done, step).wait()


def left_call(where, own, far, v_cols, upper, vectors, row_check, col_check, window):
    n_rows, n_cols = window.shape
    return pl.pallas_call(
        left_kernel,
        in_specs=[SMEM] + [VMEM] * 7 + [HBM],
        out_specs=[VMEM, VMEM, HBM],
        out_shape=[f32(1, n_rows), f32(1, n_cols), jax.ShapeDtypeStruct((n_rows, n_cols), jnp.float32)],
        scratch_shapes=[
            pltpu.VMEM((n_rows, n_cols), jnp.float32),
            pltpu.SemaphoreType.DMA((STEPS,)),
            pltpu.SemaphoreType.DMA((STEPS,)),
        ],
        name="left",
    )(where, vmem(own), vmem(far), v_cols, upper, vectors, row_check.reshape(1, n_rows), col_check.reshape(1, n_cols), window)


def right_kernel(v_ref, g_ref, u_ref, vec_ref, row_ref, col_ref, window_ref, nrow_ref, ncol_ref, out_ref, buf, sems, done):
    for step in range(STEPS):
        block_copy(window_ref, buf, sems, step).start()
    n_cols = window_ref.shape[1]
    kdim = u_ref.shape[0]
    upper = split(u_ref[...])
    g_all = g_ref[...]
    m_parts = split(mm(upper, split(g_all[:, :n_cols]), TN))
    ncol_ref[...] = col_ref[...] - mm(split(vec_ref[...]), m_parts, NN)[:1]
    lanes = g_all.shape[1] - n_cols
    extra = jnp.sum(g_all[:, n_cols:].reshape(16, kdim // 16, lanes), axis=0)
    inner = jnp.concatenate([extra[i : i + 1] for i in range(kdim // lanes)], axis=1)
    inner = split(mm(split(jnp.broadcast_to(inner, (8, kdim))), upper, NN))
    rows = window_ref.shape[0] // STEPS
    for step in range(STEPS):
        part = slice(step * rows, (step + 1) * rows)
        v_parts = split(v_ref[part])
        out = mm(v_parts, m_parts, NN)
        block_copy(window_ref, buf, sems, step).wait()
        buf[part] = buf[part] - out
        block_copy(buf, out_ref, done, step).start()
        nrow_ref[:, part] = row_ref[:, part] - mm(inner, v_parts, NT)[:1]
    for step in range(STEPS):
        block_copy(buf, out_ref, done, step).wait()


def right_call(v_rows, g_all, upper, vectors, row_part, col_part, window):
    n_rows, n_cols = window.shape
    return pl.pallas_call(
        right_kernel,
        in_specs=[VMEM] * 6 + [HBM],
        out_specs=[VMEM, VMEM, HBM],
        out_shape=[jax.ShapeDtypeStruct(shape, jnp.float32) for shape in ((1, n_rows), (1, n_cols), (n_rows, n_cols))],
        scratch_shapes=[
            pltpu.VMEM((n_rows, n_cols), jnp.float32),
            pltpu.SemaphoreType.DMA((STEPS,)),
            pltpu.SemaphoreType.DMA((STEPS,)),
        ],
        name="right",
    )(v_rows, vmem(g_all), upper, vectors, vmem(row_part), vmem(col_part), window)


def on_device(window, panel, factor, col_check, row_check):
    y, zh, core = lax.axis_index("y"), lax.axis_index("zh"), lax.axis_index("core")
    x, zl = lax.axis_index("x"), lax.axis_index("zl")
    prow = y * 4 + zh
    pcol = (x * 4 + zl) * 2 + core
    kdim = panel.shape[1]
    shard = panel.shape[0]
    n_rows, n_cols = window.shape
    upper = jnp.triu(factor)

    mine = gather(panel, ("x", "zl"), 16)
    quarter = lax.dynamic_slice_in_dim(mine, x // 2 * (n_cols // 2), n_cols // 2, 0)
    moved = lax.ppermute(quarter, AXES, transposition())
    other = swap(mine, "core", 2, 1)
    v_rows, w_part, row_part = rows_call(
        jnp.stack([core, prow * n_rows]).astype(jnp.int32),
        mine.reshape(-1, shard, kdim),
        other.reshape(-1, shard, kdim),
        window,
        row_check,
    )
    w_part = reduce_scatter(w_part, "y", 4)
    near = swap(moved, "y", 4, 1)
    w_slice = reduce_scatter(w_part, "zh", 4)

    k_rows = w_slice.shape[0]
    v_cols, keep, send, tail = cols_call(
        jnp.stack([y % 2, pcol * n_cols, core]).astype(jnp.int32),
        moved.reshape(-1, shard, kdim),
        near.reshape(-1, shard, kdim),
        col_check,
        window,
    )
    x_part = keep + swap(send, "core", 2, 1)
    small = jnp.concatenate([dot(w_slice, v_cols), tail], axis=0)
    x_part, small = reduce_both(x_part, small, "x", 4)
    both = jnp.concatenate([x_part, small], axis=0)
    total = jnp.sum(gather(both, "zl", 4).reshape((4,) + both.shape), axis=0)
    x_rows, small = total[: x_part.shape[0]], total[x_part.shape[0] :]
    y_rows = gather(dot(x_rows, upper), "x", 4)
    y_far = swap(y_rows, "core", 2, 1)

    small = small + swap(small, "core", 2, 1)
    p_slice, col_proj, sums = small[:k_rows], small[k_rows], small[k_rows + 1]
    scaled = sums / math.sqrt(N)
    vectors = jnp.concatenate([scaled[None], col_proj[None], jnp.zeros((6, kdim), jnp.float32)], axis=0)
    z_slice = dot(p_slice, upper)
    g_slice = w_slice - dot(z_slice, v_cols, ((1,), (1,)))
    z_scaled = dot(scaled[None], z_slice, ((1,), (1,)))
    lanes = 128
    owner = lax.broadcasted_iota(jnp.int32, (1, kdim), 1) // k_rows
    partial = row_part - jnp.where(owner == prow, jnp.tile(z_scaled, (1, kdim // k_rows)), 0.0)
    extra = jnp.pad(partial.reshape(kdim // lanes, lanes), ((0, k_rows - kdim // lanes), (0, 0)))
    g_all = gather(jnp.concatenate([g_slice, extra], axis=1), "zh", 4)
    g_all = gather(g_all, "y", 4)

    new_row, new_col, partly = left_call(
        core[None].astype(jnp.int32), y_rows, y_far, v_cols, upper, vectors, row_check, col_check, window
    )
    new_row, new_col, new_window = right_call(v_rows, g_all, upper, vectors, new_row, new_col, partly)
    return new_window, new_col.reshape(n_cols), new_row.reshape(n_rows)


def solution(mesh):
    fine = Mesh(mesh.devices.reshape(SIZES), AXES)
    rows, cols = ("y", "zh"), ("x", "zl", "core")
    placed = (P(rows, cols), P(AXES, None), P(), P(cols), P(rows))
    return jax.shard_map(
        on_device,
        mesh=fine,
        in_specs=placed,
        out_specs=(P(rows, cols), P(cols), P(rows)),
        check_vma=False,
    )
```

```python
import math

import jax
import jax.numpy as jnp
from jax import lax
from jax.experimental import pallas as pl
from jax.experimental.pallas import tpu as pltpu
from jax.sharding import Mesh, PartitionSpec as P


N = 16384
AXES = ("y", "zh", "x", "zl", "core")
SIZES = (4, 4, 4, 4, 2)
PREC = lax.Precision.HIGH


def dot(left, right, dims=((1,), (0,))):
    return lax.dot_general(left, right, (dims, ((), ())), precision=PREC)


def unit_lower(values, row_start):
    rows = row_start + lax.broadcasted_iota(jnp.int32, values.shape, 0)
    cols = lax.broadcasted_iota(jnp.int32, values.shape, 1)
    return jnp.where(rows > cols, values, jnp.where(rows == cols, 1.0, 0.0))


def exchange(parts, axis):
    return lax.all_to_all(parts, axis, 0, 0)


def gather(block, axis, size):
    parts = exchange(jnp.broadcast_to(block[None], (size,) + block.shape), axis)
    return parts.reshape((size * block.shape[0],) + block.shape[1:])


def reduce_scatter(block, axis, size):
    rows = block.shape[0] // size
    return jnp.sum(exchange(block.reshape(size, rows, block.shape[1]), axis), axis=0)


def reduce_both(block, small, axis, size):
    rows = block.shape[0] // size
    cut = block.reshape(size, rows, block.shape[1])
    both = jnp.concatenate([cut, jnp.broadcast_to(small[None], (size,) + small.shape)], axis=1)
    total = jnp.sum(exchange(both, axis), axis=0)
    return total[:rows], total[rows:]


def swap(block, axis, size, bit):
    return lax.ppermute(block, axis, [(i, i ^ bit) for i in range(size)])


def transposition():
    pairs = []
    for y in range(4):
        for zh in range(4):
            for x in range(4):
                for zl in range(4):
                    for core in range(2):
                        src = (((y * 4 + zh) * 4 + x) * 4 + zl) * 2 + core
                        new_y = x % 2 * 2 + core
                        dst = (((new_y * 4 + zl) * 4 + y) * 4 + zh) * 2 + x // 2
                        pairs.append((src, dst))
    return pairs


def split(value):
    high = value.astype(jnp.bfloat16)
    return high, (value - high.astype(jnp.float32)).astype(jnp.bfloat16)


def left3(value, axis):
    high, low = split(value)
    return jnp.concatenate([high, high, low], axis=axis)


def right3(value, axis):
    high, low = split(value)
    return jnp.concatenate([high, low, high], axis=axis)


def mm3(left, right, dims):
    return lax.dot_general(left, right, (dims, ((), ())), preferred_element_type=jnp.float32)


def mm(left, right, dims):
    return mm3(left3(left, dims[0][0]), right3(right, dims[1][0]), dims)


def triu(ref):
    rows = lax.broadcasted_iota(jnp.int32, ref.shape, 0)
    cols = lax.broadcasted_iota(jnp.int32, ref.shape, 1)
    return jnp.where(rows <= cols, ref[...], 0.0)


NN = ((1,), (0,))
NT = ((1,), (1,))
TN = ((0,), (0,))
STEPS = 4
LANES = 128
VMEM = pl.BlockSpec(memory_space=pltpu.VMEM)
HBM = pl.BlockSpec(memory_space=pltpu.HBM)


def near_f32(*shape):
    return pltpu.VMEM(shape, jnp.float32)


def far_f32(*shape):
    return jax.ShapeDtypeStruct(shape, jnp.float32)


def vmem(value):
    return pltpu.with_memory_space_constraint(value, pltpu.VMEM)


def staged(shape, dtype=jnp.float32):
    return [pltpu.VMEM(shape, dtype), pltpu.SemaphoreType.DMA((STEPS,))]


def block_copy(src, dst, sems, step):
    rows = src.shape[0] // STEPS
    part = pl.ds(step * rows, rows)
    return pltpu.make_async_copy(src.at[part], dst.at[part], sems.at[step])


def interleaved(lead, own, far):
    groups, shard, kdim = own.shape
    first = jnp.where(lead > 0.5, own, far)
    second = jnp.where(lead > 0.5, far, own)
    return jnp.concatenate([first, second], axis=1).reshape(2 * groups * shard, kdim)


def flag(index):
    return jnp.where(index == 0, 1.0, 0.0)


def rows_kernel(mine_ref, other_ref, window_ref, v_ref, w_ref, buf, sems):
    for step in range(STEPS):
        block_copy(window_ref, buf, sems, step).start()
    lead = flag(lax.axis_index("core"))
    start = (lax.axis_index("y") * 4 + lax.axis_index("zh")) * v_ref.shape[0]
    groups, rows = mine_ref.shape[0] // STEPS, v_ref.shape[0] // STEPS
    for step in range(STEPS):
        mine, other = (ref[step * groups : (step + 1) * groups] for ref in (mine_ref, other_ref))
        block = unit_lower(interleaved(lead, mine, other), start + step * rows)
        part = slice(step * rows, (step + 1) * rows)
        v_ref[part] = block
        block_copy(window_ref, buf, sems, step).wait()
        w_part = mm(block, buf[part], TN)
        if step == 0:
            w_ref[...] = w_part
        else:
            w_ref[...] += w_part


def rows_call(mine, other, window):
    n_rows, n_cols = window.shape
    kdim = mine.shape[2]
    return pl.pallas_call(
        rows_kernel,
        in_specs=[VMEM, VMEM, HBM],
        out_specs=[VMEM] * 2,
        out_shape=[near_f32(n_rows, kdim), near_f32(kdim, n_cols)],
        scratch_shapes=staged((n_rows, n_cols)),
        name="rows",
    )(vmem(mine), vmem(other), window)


def cols_kernel(own_ref, far_ref, check_ref, window_ref, v_ref, keep_ref, send_ref, tail_ref, buf, sems):
    for step in range(STEPS):
        block_copy(window_ref, buf, sems, step).start()
    core = lax.axis_index("core")
    pcol = (lax.axis_index("x") * 4 + lax.axis_index("zl")) * 2 + core
    lead = flag(lax.axis_index("y") % 2)
    block = unit_lower(interleaved(lead, own_ref[...], far_ref[...]), pcol * v_ref.shape[0])
    v_ref[...] = block
    right = right3(block, 0)
    line = lax.broadcasted_iota(jnp.int32, (8, check_ref.shape[1]), 0)
    tail = jnp.where(line == 0, check_ref[...], jnp.where(line == 1, 1.0, 0.0))
    half, rows = STEPS // 2, window_ref.shape[0] // STEPS
    for step in range(STEPS):
        block_copy(window_ref, buf, sems, step).wait()
        chunk = buf[step * rows : (step + 1) * rows]
        if step == 0:
            chunk = jnp.concatenate([chunk, tail], axis=0)
        x = mm3(left3(chunk, 1), right, NN)
        if step == 0:
            tail_ref[...] = x[rows:]
            x = x[:rows]
        part = slice(step % half * rows, (step % half + 1) * rows)

        @pl.when(core == step // half)
        def _():
            keep_ref[part] = x

        @pl.when(core != step // half)
        def _():
            send_ref[part] = x


def cols_call(own, far, check, window):
    n_rows, n_cols = window.shape
    kdim = own.shape[2]
    half = near_f32(n_rows // 2, kdim)
    return pl.pallas_call(
        cols_kernel,
        in_specs=[VMEM, VMEM, VMEM, HBM],
        out_specs=[VMEM] * 4,
        out_shape=[near_f32(n_cols, kdim), half, half, near_f32(8, kdim)],
        scratch_shapes=staged((n_rows, n_cols)),
        name="cols",
    )(vmem(own), vmem(far), check.reshape(1, n_cols), window)


def prep_kernel(v_ref, u_ref, check_ref, turned_ref, part_ref):
    upper = right3(triu(u_ref), 1)
    rows = v_ref.shape[0] // STEPS
    total = None
    for step in range(STEPS):
        part = slice(step * rows, (step + 1) * rows)
        block = v_ref[part]
        turned_ref[part] = left3(mm3(left3(block, 1), upper, NT), 1)
        sums = mm(jnp.broadcast_to(check_ref[:, part], (8, rows)), block, NN)
        total = sums if step == 0 else total + sums
    part_ref[...] = total[:1]


def prep_call(v_rows, factor, check):
    n_rows, kdim = v_rows.shape
    return pl.pallas_call(
        prep_kernel,
        in_specs=[VMEM] * 3,
        out_specs=[VMEM] * 2,
        out_shape=[jax.ShapeDtypeStruct((n_rows, 3 * kdim), jnp.bfloat16), far_f32(1, kdim)],
        name="prep",
    )(v_rows, factor, check.reshape(1, n_rows))


def spread_kernel(parts_ref, u_ref, y_ref, small_ref):
    total = jnp.sum(parts_ref[...], axis=0)
    rows = y_ref.shape[1]
    y_rows = mm(total[:rows], triu(u_ref), NN)
    for j in range(y_ref.shape[0]):
        y_ref[j] = y_rows
    small_ref[...] = total[rows:]


def spread_call(parts, factor, rows):
    size, tall, kdim = parts.shape
    return pl.pallas_call(
        spread_kernel,
        in_specs=[VMEM] * 2,
        out_specs=[VMEM] * 2,
        out_shape=[near_f32(size, rows, kdim), near_f32(tall - rows, kdim)],
        name="spread",
    )(vmem(parts), factor)


def slice_kernel(own_ref, far_ref, w_ref, c_ref, u_ref, part_ref, g_ref, vec_ref):
    k_rows, n_cols = w_ref.shape
    kdim = u_ref.shape[0]
    small = own_ref[...] + far_ref[...]
    upper = triu(u_ref)
    scaled = small[k_rows + 1 : k_rows + 2] / math.sqrt(N)
    line = lax.broadcasted_iota(jnp.int32, (8, kdim), 0)
    turned = mm(jnp.broadcast_to(scaled, (8, kdim)), upper, NT)
    vec_ref[...] = jnp.where(line == 0, scaled, jnp.where(line == 1, small[k_rows : k_rows + 1], jnp.where(line == 2, turned, 0.0)))
    z = mm(small[:k_rows], upper, NN)
    g = w_ref[...] - mm(z, c_ref[...], NT)
    prow = lax.axis_index("y") * 4 + lax.axis_index("zh")
    owner = prow * k_rows + lax.broadcasted_iota(jnp.int32, (k_rows, kdim), 0)
    mine = lax.broadcasted_iota(jnp.int32, (k_rows, kdim), 1) == owner
    z_scaled = jnp.sum(z * scaled, axis=1, keepdims=True)
    partial = part_ref[...] - jnp.sum(jnp.where(mine, z_scaled, 0.0), axis=0, keepdims=True)
    row = lax.broadcasted_iota(jnp.int32, (k_rows, LANES), 0)
    extra = jnp.zeros((k_rows, LANES), jnp.float32)
    for i in range(kdim // LANES):
        extra = jnp.where(row == i, partial[:, i * LANES : (i + 1) * LANES], extra)
    for j in range(g_ref.shape[0]):
        g_ref[j, :, :n_cols] = g
        g_ref[j, :, n_cols:] = extra


def slice_call(own, far, w_slice, v_cols, factor, part):
    k_rows, n_cols = w_slice.shape
    kdim = factor.shape[0]
    return pl.pallas_call(
        slice_kernel,
        in_specs=[VMEM] * 6,
        out_specs=[VMEM] * 2,
        out_shape=[near_f32(4, k_rows, n_cols + LANES), near_f32(8, kdim)],
        name="slice",
    )(vmem(own), vmem(far), vmem(w_slice), vmem(v_cols), factor, part)


def left_kernel(own_ref, far_ref, c_ref, u_ref, vec_ref, row_ref, col_ref, window_ref, nrow_ref, ncol_ref, out_ref, buf, sems, done):
    for step in range(STEPS):
        block_copy(window_ref, buf, sems, step).start()
    right = right3(c_ref[...], 1)
    vec = vec_ref[...]
    turned = mm(vec, triu(u_ref), NN)
    ncol_ref[...] = col_ref[...] - mm3(left3(turned, 1), right, NT)[1:2]
    vec = left3(vec, 1)
    half, rows = STEPS // 2, window_ref.shape[0] // STEPS
    lead = flag(lax.axis_index("core"))
    for step in range(STEPS):
        piece = slice(step % half * rows, (step % half + 1) * rows)
        mine = lead if step < half else 1.0 - lead
        block = jnp.where(mine > 0.5, own_ref[piece], far_ref[piece])
        part = slice(step * rows, (step + 1) * rows)
        out = mm3(left3(block, 1), right, NT)
        block_copy(window_ref, buf, sems, step).wait()
        buf[part] = buf[part] - out
        block_copy(buf, out_ref, done, step).start()
        nrow_ref[:, part] = row_ref[:, part] - mm3(vec, right3(block, 1), NT)[:1]
    for step in range(STEPS):
        block_copy(buf, out_ref, done, step).wait()


def left_call(own, far, v_cols, factor, vectors, row_check, col_check, window):
    n_rows, n_cols = window.shape
    return pl.pallas_call(
        left_kernel,
        in_specs=[VMEM] * 7 + [HBM],
        out_specs=[VMEM, VMEM, HBM],
        out_shape=[near_f32(1, n_rows), near_f32(1, n_cols), far_f32(n_rows, n_cols)],
        scratch_shapes=staged((n_rows, n_cols)) + [pltpu.SemaphoreType.DMA((STEPS,))],
        name="left",
    )(
        vmem(own),
        vmem(far),
        vmem(v_cols),
        factor,
        vmem(vectors),
        row_check.reshape(1, n_rows),
        col_check.reshape(1, n_cols),
        window,
    )


def right_kernel(g_ref, vec_ref, row_ref, col_ref, turned_ref, window_ref, nrow_ref, ncol_ref, out_ref, tbuf, tsems, buf, sems, done):
    for step in range(STEPS):
        block_copy(turned_ref, tbuf, tsems, step).start()
        block_copy(window_ref, buf, sems, step).start()
    n_cols = window_ref.shape[1]
    kdim = g_ref.shape[0]
    g_all = g_ref[...]
    extra = jnp.sum(g_all[:, n_cols:].reshape(16, kdim // 16, LANES), axis=0)
    inner = jnp.concatenate([extra[i : i + 1] for i in range(kdim // LANES)], axis=1)
    inner = jnp.broadcast_to(inner, (LANES, kdim)).T
    right = right3(jnp.concatenate([g_all[:, :n_cols], inner], axis=1), 0)
    rows = window_ref.shape[0] // STEPS
    for step in range(STEPS):
        part = slice(step * rows, (step + 1) * rows)
        block_copy(turned_ref, tbuf, tsems, step).wait()
        left = tbuf[part]
        if step == 0:
            left = jnp.concatenate([left, left3(vec_ref[...], 1)], axis=0)
        out = mm3(left, right, NN)
        if step == 0:
            ncol_ref[...] = col_ref[...] - out[rows + 2 : rows + 3, :n_cols]
            out = out[:rows]
        block_copy(window_ref, buf, sems, step).wait()
        buf[part] = buf[part] - out[:, :n_cols]
        block_copy(buf, out_ref, done, step).start()
        nrow_ref[:, part] = row_ref[:, part] - out[:, n_cols:].T[:1]
    for step in range(STEPS):
        block_copy(buf, out_ref, done, step).wait()


def right_call(g_all, vectors, row_part, col_part, turned, window):
    n_rows, n_cols = window.shape
    return pl.pallas_call(
        right_kernel,
        in_specs=[VMEM] * 4 + [HBM] * 2,
        out_specs=[VMEM, VMEM, HBM],
        out_shape=[far_f32(1, n_rows), far_f32(1, n_cols), far_f32(n_rows, n_cols)],
        scratch_shapes=staged(turned.shape, turned.dtype) + staged((n_rows, n_cols)) + [pltpu.SemaphoreType.DMA((STEPS,))],
        name="right",
    )(vmem(g_all), vmem(vectors), vmem(row_part), vmem(col_part), turned, window)


def on_device(window, panel, factor, col_check, row_check):
    x = lax.axis_index("x")
    kdim = panel.shape[1]
    shard = panel.shape[0]
    n_rows, n_cols = window.shape

    line = gather(panel, "zl", 4)
    mine = gather(line, "x", 4)
    quarter = lax.dynamic_slice_in_dim(mine, x // 2 * (n_cols // 2), n_cols // 2, 0)
    moved = lax.ppermute(quarter, AXES, transposition())
    other = swap(mine, "core", 2, 1)
    v_rows, w_part = rows_call(mine.reshape(-1, shard, kdim), other.reshape(-1, shard, kdim), window)
    w_part = reduce_scatter(w_part, "y", 4)
    near = swap(moved, "y", 4, 1)
    w_slice = reduce_scatter(w_part, "zh", 4)

    v_cols, keep, send, tail = cols_call(moved.reshape(-1, shard, kdim), near.reshape(-1, shard, kdim), col_check, window)
    x_part = keep + swap(send, "core", 2, 1)
    small = jnp.concatenate([dot(w_slice, v_cols), tail], axis=0)
    x_part, small = reduce_both(x_part, small, "x", 4)
    both = jnp.concatenate([x_part, small], axis=0)
    parts = gather(both, "zl", 4).reshape((4,) + both.shape)
    turned, row_part = prep_call(v_rows, factor, row_check)
    y_parts, small = spread_call(parts, factor, x_part.shape[0])
    y_rows = exchange(y_parts, "x").reshape(n_rows // 2, kdim)
    y_far = swap(y_rows, "core", 2, 1)
    small_far = swap(small, "core", 2, 1)
    g_parts, vectors = slice_call(small, small_far, w_slice, v_cols, factor, row_part)
    g_some = exchange(g_parts, "zh").reshape(-1, n_cols + LANES)
    g_all = gather(g_some, "y", 4)

    new_row, new_col, partly = left_call(y_rows, y_far, v_cols, factor, vectors, row_check, col_check, window)
    new_row, new_col, new_window = right_call(g_all, vectors, new_row, new_col, turned, partly)
    return new_window, new_col.reshape(n_cols), new_row.reshape(n_rows)


def solution(mesh):
    fine = Mesh(mesh.devices.reshape(SIZES), AXES)
    rows, cols = ("y", "zh"), ("x", "zl", "core")
    placed = (P(rows, cols), P(AXES, None), P(), P(cols), P(rows))
    return jax.shard_map(
        on_device,
        mesh=fine,
        in_specs=placed,
        out_specs=(P(rows, cols), P(cols), P(rows)),
        check_vma=False,
    )
```

```python
import math

import jax
import jax.numpy as jnp
from jax import lax
from jax.experimental import pallas as pl
from jax.experimental.pallas import tpu as pltpu
from jax.sharding import Mesh, PartitionSpec as P


N = 16384
AXES = ("y", "zh", "x", "zl", "core")
SIZES = (4, 4, 4, 4, 2)
PREC = lax.Precision.HIGH


def dot(left, right, dims=((1,), (0,))):
    return lax.dot_general(left, right, (dims, ((), ())), precision=PREC)


def unit_lower(values, row_start):
    rows = row_start + lax.broadcasted_iota(jnp.int32, values.shape, 0)
    cols = lax.broadcasted_iota(jnp.int32, values.shape, 1)
    return jnp.where(rows > cols, values, jnp.where(rows == cols, 1.0, 0.0))


def exchange(parts, axis):
    return lax.all_to_all(parts, axis, 0, 0)


def gather(block, axis, size):
    parts = exchange(jnp.broadcast_to(block[None], (size,) + block.shape), axis)
    return parts.reshape((size * block.shape[0],) + block.shape[1:])


def reduce_scatter(block, axis, size):
    rows = block.shape[0] // size
    return jnp.sum(exchange(block.reshape(size, rows, block.shape[1]), axis), axis=0)


def reduce_both(block, small, axis, size):
    rows = block.shape[0] // size
    cut = block.reshape(size, rows, block.shape[1])
    both = jnp.concatenate([cut, jnp.broadcast_to(small[None], (size,) + small.shape)], axis=1)
    total = jnp.sum(exchange(both, axis), axis=0)
    return total[:rows], total[rows:]


def swap(block, axis, size, bit):
    return lax.ppermute(block, axis, [(i, i ^ bit) for i in range(size)])


def halved(block, axis, size, bit):
    high = lax.axis_index(axis) // bit % 2
    rows = block.shape[0] // 2
    keep = lax.dynamic_slice_in_dim(block, high * rows, rows, 0)
    send = lax.dynamic_slice_in_dim(block, (1 - high) * rows, rows, 0)
    return keep + swap(send, axis, size, bit)


def doubled(block, axis, size, bit, dim):
    other = swap(block, axis, size, bit)
    low = lax.axis_index(axis) // bit % 2 == 0
    pair = [jnp.where(low, block, other), jnp.where(low, other, block)]
    return jnp.stack(pair, axis=dim)


def transposition():
    pairs = []
    for y in range(4):
        for zh in range(4):
            for x in range(4):
                for zl in range(4):
                    for core in range(2):
                        src = (((y * 4 + zh) * 4 + x) * 4 + zl) * 2 + core
                        new_y = x % 2 * 2 + core
                        dst = (((new_y * 4 + zl) * 4 + y) * 4 + zh) * 2 + x // 2
                        pairs.append((src, dst))
    return pairs


def split(value):
    high = value.astype(jnp.bfloat16)
    return high, (value - high.astype(jnp.float32)).astype(jnp.bfloat16)


def left3(value, axis):
    high, low = split(value)
    return jnp.concatenate([high, high, low], axis=axis)


def right3(value, axis):
    high, low = split(value)
    return jnp.concatenate([high, low, high], axis=axis)


def mm3(left, right, dims):
    return lax.dot_general(left, right, (dims, ((), ())), preferred_element_type=jnp.float32)


def mm(left, right, dims):
    return mm3(left3(left, dims[0][0]), right3(right, dims[1][0]), dims)


def triu(ref):
    rows = lax.broadcasted_iota(jnp.int32, ref.shape, 0)
    cols = lax.broadcasted_iota(jnp.int32, ref.shape, 1)
    return jnp.where(rows <= cols, ref[...], 0.0)


NN = ((1,), (0,))
NT = ((1,), (1,))
TN = ((0,), (0,))
STEPS = 4
LANES = 128
VMEM = pl.BlockSpec(memory_space=pltpu.VMEM)
HBM = pl.BlockSpec(memory_space=pltpu.HBM)


def near_f32(*shape):
    return pltpu.VMEM(shape, jnp.float32)


def far_f32(*shape):
    return jax.ShapeDtypeStruct(shape, jnp.float32)


def vmem(value):
    return pltpu.with_memory_space_constraint(value, pltpu.VMEM)


def staged(shape, dtype=jnp.float32):
    return [pltpu.VMEM(shape, dtype), pltpu.SemaphoreType.DMA((STEPS,))]


def block_copy(src, dst, sems, step):
    rows = src.shape[0] // STEPS
    part = pl.ds(step * rows, rows)
    return pltpu.make_async_copy(src.at[part], dst.at[part], sems.at[step])


def interleaved(lead, own, far):
    groups, shard, kdim = own.shape
    first = jnp.where(lead > 0.5, own, far)
    second = jnp.where(lead > 0.5, far, own)
    return jnp.concatenate([first, second], axis=1).reshape(2 * groups * shard, kdim)


def flag(index):
    return jnp.where(index == 0, 1.0, 0.0)


def rows_kernel(mine_ref, other_ref, window_ref, v_ref, w_ref, buf, sems):
    for step in range(STEPS):
        block_copy(window_ref, buf, sems, step).start()
    lead = flag(lax.axis_index("core"))
    start = (lax.axis_index("y") * 4 + lax.axis_index("zh")) * v_ref.shape[0]
    groups, rows = mine_ref.shape[0] // STEPS, v_ref.shape[0] // STEPS
    for step in range(STEPS):
        mine, other = (ref[step * groups : (step + 1) * groups] for ref in (mine_ref, other_ref))
        block = unit_lower(interleaved(lead, mine, other), start + step * rows)
        part = slice(step * rows, (step + 1) * rows)
        v_ref[part] = block
        block_copy(window_ref, buf, sems, step).wait()
        w_part = mm(block, buf[part], TN)
        if step == 0:
            w_ref[...] = w_part
        else:
            w_ref[...] += w_part


def rows_call(mine, other, window):
    n_rows, n_cols = window.shape
    kdim = mine.shape[2]
    return pl.pallas_call(
        rows_kernel,
        in_specs=[VMEM, VMEM, HBM],
        out_specs=[VMEM] * 2,
        out_shape=[near_f32(n_rows, kdim), near_f32(kdim, n_cols)],
        scratch_shapes=staged((n_rows, n_cols)),
        name="rows",
    )(vmem(mine), vmem(other), window)


def cols_kernel(own_ref, far_ref, check_ref, window_ref, v_ref, keep_ref, send_ref, tail_ref, buf, sems):
    for step in range(STEPS):
        block_copy(window_ref, buf, sems, step).start()
    core = lax.axis_index("core")
    pcol = (lax.axis_index("x") * 4 + lax.axis_index("zl")) * 2 + core
    lead = flag(lax.axis_index("y") % 2)
    block = unit_lower(interleaved(lead, own_ref[...], far_ref[...]), pcol * v_ref.shape[0])
    v_ref[...] = block
    right = right3(block, 0)
    line = lax.broadcasted_iota(jnp.int32, (8, check_ref.shape[1]), 0)
    tail = jnp.where(line == 0, check_ref[...], jnp.where(line == 1, 1.0, 0.0))
    half, rows = STEPS // 2, window_ref.shape[0] // STEPS
    for step in range(STEPS):
        block_copy(window_ref, buf, sems, step).wait()
        chunk = buf[step * rows : (step + 1) * rows]
        if step == 0:
            chunk = jnp.concatenate([chunk, tail], axis=0)
        x = mm3(left3(chunk, 1), right, NN)
        if step == 0:
            tail_ref[...] = x[rows:]
            x = x[:rows]
        part = slice(step % half * rows, (step % half + 1) * rows)

        @pl.when(core == step // half)
        def _():
            keep_ref[part] = x

        @pl.when(core != step // half)
        def _():
            send_ref[part] = x


def cols_call(own, far, check, window):
    n_rows, n_cols = window.shape
    kdim = own.shape[2]
    half = near_f32(n_rows // 2, kdim)
    return pl.pallas_call(
        cols_kernel,
        in_specs=[VMEM, VMEM, VMEM, HBM],
        out_specs=[VMEM] * 4,
        out_shape=[near_f32(n_cols, kdim), half, half, near_f32(8, kdim)],
        scratch_shapes=staged((n_rows, n_cols)),
        name="cols",
    )(vmem(own), vmem(far), check.reshape(1, n_cols), window)


def prep_kernel(v_ref, u_ref, check_ref, turned_ref, part_ref):
    upper = right3(triu(u_ref), 1)
    rows = v_ref.shape[0] // STEPS
    total = None
    for step in range(STEPS):
        part = slice(step * rows, (step + 1) * rows)
        block = v_ref[part]
        turned_ref[part] = left3(mm3(left3(block, 1), upper, NT), 1)
        sums = mm(jnp.broadcast_to(check_ref[:, part], (8, rows)), block, NN)
        total = sums if step == 0 else total + sums
    part_ref[...] = total[:1]


def prep_call(v_rows, factor, check):
    n_rows, kdim = v_rows.shape
    return pl.pallas_call(
        prep_kernel,
        in_specs=[VMEM] * 3,
        out_specs=[VMEM] * 2,
        out_shape=[jax.ShapeDtypeStruct((n_rows, 3 * kdim), jnp.bfloat16), far_f32(1, kdim)],
        name="prep",
    )(v_rows, factor, check.reshape(1, n_rows))


def slice_kernel(own_ref, far_ref, w_ref, c_ref, u_ref, part_ref, g_ref, vec_ref):
    k_rows, n_cols = w_ref.shape
    kdim = u_ref.shape[0]
    small = own_ref[...] + far_ref[...]
    upper = triu(u_ref)
    scaled = small[k_rows + 1 : k_rows + 2] / math.sqrt(N)
    line = lax.broadcasted_iota(jnp.int32, (8, kdim), 0)
    turned = mm(jnp.broadcast_to(scaled, (8, kdim)), upper, NT)
    vec_ref[...] = jnp.where(line == 0, scaled, jnp.where(line == 1, small[k_rows : k_rows + 1], jnp.where(line == 2, turned, 0.0)))
    z = mm(small[:k_rows], upper, NN)
    g = w_ref[...] - mm(z, c_ref[...], NT)
    prow = lax.axis_index("y") * 4 + lax.axis_index("zh")
    owner = prow * k_rows + lax.broadcasted_iota(jnp.int32, (k_rows, kdim), 0)
    mine = lax.broadcasted_iota(jnp.int32, (k_rows, kdim), 1) == owner
    z_scaled = jnp.sum(z * scaled, axis=1, keepdims=True)
    partial = part_ref[...] - jnp.sum(jnp.where(mine, z_scaled, 0.0), axis=0, keepdims=True)
    row = lax.broadcasted_iota(jnp.int32, (k_rows, LANES), 0)
    extra = jnp.zeros((k_rows, LANES), jnp.float32)
    for i in range(kdim // LANES):
        extra = jnp.where(row == i, partial[:, i * LANES : (i + 1) * LANES], extra)
    g_ref[:, :n_cols] = g
    g_ref[:, n_cols:] = extra


def slice_call(own, far, w_slice, v_cols, factor, part):
    k_rows, n_cols = w_slice.shape
    kdim = factor.shape[0]
    return pl.pallas_call(
        slice_kernel,
        in_specs=[VMEM] * 6,
        out_specs=[VMEM] * 2,
        out_shape=[near_f32(k_rows, n_cols + LANES), near_f32(8, kdim)],
        name="slice",
    )(vmem(own), vmem(far), vmem(w_slice), vmem(v_cols), factor, part)


def left_kernel(own_ref, far_ref, c_ref, u_ref, vec_ref, row_ref, col_ref, window_ref, nrow_ref, ncol_ref, out_ref, buf, sems, done):
    for step in range(STEPS):
        block_copy(window_ref, buf, sems, step).start()
    right = right3(c_ref[...], 1)
    vec = vec_ref[...]
    turned = mm(vec, triu(u_ref), NN)
    ncol_ref[...] = col_ref[...] - mm3(left3(turned, 1), right, NT)[1:2]
    vec = left3(vec, 1)
    half, rows = STEPS // 2, window_ref.shape[0] // STEPS
    lead = flag(lax.axis_index("core"))
    for step in range(STEPS):
        piece = slice(step % half * rows, (step % half + 1) * rows)
        mine = lead if step < half else 1.0 - lead
        block = jnp.where(mine > 0.5, own_ref[piece], far_ref[piece])
        part = slice(step * rows, (step + 1) * rows)
        out = mm3(left3(block, 1), right, NT)
        block_copy(window_ref, buf, sems, step).wait()
        buf[part] = buf[part] - out
        block_copy(buf, out_ref, done, step).start()
        nrow_ref[:, part] = row_ref[:, part] - mm3(vec, right3(block, 1), NT)[:1]
    for step in range(STEPS):
        block_copy(buf, out_ref, done, step).wait()


def left_call(own, far, v_cols, factor, vectors, row_check, col_check, window):
    n_rows, n_cols = window.shape
    return pl.pallas_call(
        left_kernel,
        in_specs=[VMEM] * 7 + [HBM],
        out_specs=[VMEM, VMEM, HBM],
        out_shape=[near_f32(1, n_rows), near_f32(1, n_cols), far_f32(n_rows, n_cols)],
        scratch_shapes=staged((n_rows, n_cols)) + [pltpu.SemaphoreType.DMA((STEPS,))],
        name="left",
    )(
        vmem(own),
        vmem(far),
        vmem(v_cols),
        factor,
        vmem(vectors),
        row_check.reshape(1, n_rows),
        col_check.reshape(1, n_cols),
        window,
    )


def right_kernel(g_ref, vec_ref, row_ref, col_ref, turned_ref, window_ref, nrow_ref, ncol_ref, out_ref, tbuf, tsems, buf, sems, done):
    for step in range(STEPS):
        block_copy(turned_ref, tbuf, tsems, step).start()
        block_copy(window_ref, buf, sems, step).start()
    n_cols = window_ref.shape[1]
    kdim = g_ref.shape[0]
    g_all = g_ref[...]
    extra = jnp.sum(g_all[:, n_cols:].reshape(16, kdim // 16, LANES), axis=0)
    inner = jnp.concatenate([extra[i : i + 1] for i in range(kdim // LANES)], axis=1)
    inner = jnp.broadcast_to(inner, (LANES, kdim)).T
    right = right3(jnp.concatenate([g_all[:, :n_cols], inner], axis=1), 0)
    rows = window_ref.shape[0] // STEPS
    for step in range(STEPS):
        part = slice(step * rows, (step + 1) * rows)
        block_copy(turned_ref, tbuf, tsems, step).wait()
        left = tbuf[part]
        if step == 0:
            left = jnp.concatenate([left, left3(vec_ref[...], 1)], axis=0)
        out = mm3(left, right, NN)
        if step == 0:
            ncol_ref[...] = col_ref[...] - out[rows + 2 : rows + 3, :n_cols]
            out = out[:rows]
        block_copy(window_ref, buf, sems, step).wait()
        buf[part] = buf[part] - out[:, :n_cols]
        block_copy(buf, out_ref, done, step).start()
        nrow_ref[:, part] = row_ref[:, part] - out[:, n_cols:].T[:1]
    for step in range(STEPS):
        block_copy(buf, out_ref, done, step).wait()


def right_call(g_all, vectors, row_part, col_part, turned, window):
    n_rows, n_cols = window.shape
    return pl.pallas_call(
        right_kernel,
        in_specs=[VMEM] * 4 + [HBM] * 2,
        out_specs=[VMEM, VMEM, HBM],
        out_shape=[far_f32(1, n_rows), far_f32(1, n_cols), far_f32(n_rows, n_cols)],
        scratch_shapes=staged(turned.shape, turned.dtype) + staged((n_rows, n_cols)) + [pltpu.SemaphoreType.DMA((STEPS,))],
        name="right",
    )(vmem(g_all), vmem(vectors), vmem(row_part), vmem(col_part), turned, window)


def on_device(window, panel, factor, col_check, row_check):
    x = lax.axis_index("x")
    kdim = panel.shape[1]
    shard = panel.shape[0]
    n_rows, n_cols = window.shape

    line = gather(panel, "zl", 4)
    mine = gather(line, "x", 4)
    quarter = lax.dynamic_slice_in_dim(mine, x // 2 * (n_cols // 2), n_cols // 2, 0)
    moved = lax.ppermute(quarter, AXES, transposition())
    other = swap(mine, "core", 2, 1)
    v_rows, w_part = rows_call(mine.reshape(-1, shard, kdim), other.reshape(-1, shard, kdim), window)
    w_part = reduce_scatter(w_part, "y", 4)
    near = swap(moved, "y", 4, 1)
    w_part = halved(w_part, "zh", 4, 2)
    w_slice = halved(w_part, "zh", 4, 1)

    v_cols, keep, send, tail = cols_call(moved.reshape(-1, shard, kdim), near.reshape(-1, shard, kdim), col_check, window)
    x_part = keep + swap(send, "core", 2, 1)
    small = jnp.concatenate([dot(w_slice, v_cols), tail], axis=0)
    x_part, small = reduce_both(x_part, small, "x", 4)
    both = jnp.concatenate([x_part, small], axis=0)
    total = jnp.sum(gather(both, "zl", 4).reshape((4,) + both.shape), axis=0)
    turned, row_part = prep_call(v_rows, factor, row_check)
    tall = x_part.shape[0]
    small = total[tall:]
    y_rows = gather(dot(total[:tall], jnp.triu(factor)), "x", 4)
    y_far = swap(y_rows, "core", 2, 1)
    small_far = swap(small, "core", 2, 1)
    g_part, vectors = slice_call(small, small_far, w_slice, v_cols, factor, row_part)
    g_some = doubled(g_part, "zh", 4, 2, 0)
    g_some = doubled(g_some, "zh", 4, 1, 1).reshape(-1, n_cols + LANES)
    g_all = gather(g_some, "y", 4)

    new_row, new_col, partly = left_call(y_rows, y_far, v_cols, factor, vectors, row_check, col_check, window)
    new_row, new_col, new_window = right_call(g_all, vectors, new_row, new_col, turned, partly)
    return new_window, new_col.reshape(n_cols), new_row.reshape(n_rows)


def solution(mesh):
    fine = Mesh(mesh.devices.reshape(SIZES), AXES)
    rows, cols = ("y", "zh"), ("x", "zl", "core")
    placed = (P(rows, cols), P(AXES, None), P(), P(cols), P(rows))
    return jax.shard_map(
        on_device,
        mesh=fine,
        in_specs=placed,
        out_specs=(P(rows, cols), P(cols), P(rows)),
        check_vma=False,
    )
```

```python
import math

import jax
import jax.numpy as jnp
from jax import lax
from jax.experimental import pallas as pl
from jax.experimental.pallas import tpu as pltpu
from jax.sharding import Mesh, PartitionSpec as P


N = 16384
AXES = ("y", "zh", "x", "zl", "core")
SIZES = (4, 4, 4, 4, 2)
PREC = lax.Precision.HIGH


def dot(left, right, dims=((1,), (0,))):
    return lax.dot_general(left, right, (dims, ((), ())), precision=PREC)


def unit_lower(values, row_start):
    rows = row_start + lax.broadcasted_iota(jnp.int32, values.shape, 0)
    cols = lax.broadcasted_iota(jnp.int32, values.shape, 1)
    return jnp.where(rows > cols, values, jnp.where(rows == cols, 1.0, 0.0))


def exchange(parts, axis):
    return lax.all_to_all(parts, axis, 0, 0)


def gather(block, axis, size):
    parts = exchange(jnp.broadcast_to(block[None], (size,) + block.shape), axis)
    return parts.reshape((size * block.shape[0],) + block.shape[1:])


def reduce_scatter(block, axis, size):
    rows = block.shape[0] // size
    return jnp.sum(exchange(block.reshape(size, rows, block.shape[1]), axis), axis=0)


def reduce_both(block, small, axis, size):
    rows = block.shape[0] // size
    cut = block.reshape(size, rows, block.shape[1])
    both = jnp.concatenate([cut, jnp.broadcast_to(small[None], (size,) + small.shape)], axis=1)
    total = jnp.sum(exchange(both, axis), axis=0)
    return total[:rows], total[rows:]


def swap(block, axis, size, bit):
    return lax.ppermute(block, axis, [(i, i ^ bit) for i in range(size)])


def transposition():
    pairs = []
    for y in range(4):
        for zh in range(4):
            for x in range(4):
                for zl in range(4):
                    for core in range(2):
                        src = (((y * 4 + zh) * 4 + x) * 4 + zl) * 2 + core
                        new_y = x % 2 * 2 + core
                        dst = (((new_y * 4 + zl) * 4 + y) * 4 + zh) * 2 + x // 2
                        pairs.append((src, dst))
    return pairs


def split(value):
    high = value.astype(jnp.bfloat16)
    return high, (value - high.astype(jnp.float32)).astype(jnp.bfloat16)


def left3(value, axis):
    high, low = split(value)
    return jnp.concatenate([high, high, low], axis=axis)


def right3(value, axis):
    high, low = split(value)
    return jnp.concatenate([high, low, high], axis=axis)


def mm3(left, right, dims):
    return lax.dot_general(left, right, (dims, ((), ())), preferred_element_type=jnp.float32)


def mm(left, right, dims):
    return mm3(left3(left, dims[0][0]), right3(right, dims[1][0]), dims)


def triu(ref):
    rows = lax.broadcasted_iota(jnp.int32, ref.shape, 0)
    cols = lax.broadcasted_iota(jnp.int32, ref.shape, 1)
    return jnp.where(rows <= cols, ref[...], 0.0)


NN = ((1,), (0,))
NT = ((1,), (1,))
TN = ((0,), (0,))
STEPS = 4
LANES = 128
VMEM = pl.BlockSpec(memory_space=pltpu.VMEM)
HBM = pl.BlockSpec(memory_space=pltpu.HBM)


def near_f32(*shape):
    return pltpu.VMEM(shape, jnp.float32)


def far_f32(*shape):
    return jax.ShapeDtypeStruct(shape, jnp.float32)


def vmem(value):
    return pltpu.with_memory_space_constraint(value, pltpu.VMEM)


def staged(shape, dtype=jnp.float32):
    return [pltpu.VMEM(shape, dtype), pltpu.SemaphoreType.DMA((STEPS,))]


def block_copy(src, dst, sems, step):
    rows = src.shape[0] // STEPS
    part = pl.ds(step * rows, rows)
    return pltpu.make_async_copy(src.at[part], dst.at[part], sems.at[step])


def interleaved(lead, own, far):
    groups, shard, kdim = own.shape
    first = jnp.where(lead > 0.5, own, far)
    second = jnp.where(lead > 0.5, far, own)
    return jnp.concatenate([first, second], axis=1).reshape(2 * groups * shard, kdim)


def flag(index):
    return jnp.where(index == 0, 1.0, 0.0)


def rows_kernel(mine_ref, other_ref, window_ref, v_ref, w_ref, buf, sems):
    for step in range(STEPS):
        block_copy(window_ref, buf, sems, step).start()
    lead = flag(lax.axis_index("core"))
    start = (lax.axis_index("y") * 4 + lax.axis_index("zh")) * v_ref.shape[0]
    groups, rows = mine_ref.shape[0] // STEPS, v_ref.shape[0] // STEPS
    for step in range(STEPS):
        mine, other = (ref[step * groups : (step + 1) * groups] for ref in (mine_ref, other_ref))
        block = unit_lower(interleaved(lead, mine, other), start + step * rows)
        part = slice(step * rows, (step + 1) * rows)
        v_ref[part] = block
        block_copy(window_ref, buf, sems, step).wait()
        w_part = mm(block, buf[part], TN)
        if step == 0:
            w_ref[...] = w_part
        else:
            w_ref[...] += w_part


def rows_call(mine, other, window):
    n_rows, n_cols = window.shape
    kdim = mine.shape[2]
    return pl.pallas_call(
        rows_kernel,
        in_specs=[VMEM, VMEM, HBM],
        out_specs=[VMEM] * 2,
        out_shape=[near_f32(n_rows, kdim), near_f32(kdim, n_cols)],
        scratch_shapes=staged((n_rows, n_cols)),
        name="rows",
    )(vmem(mine), vmem(other), window)


def cols_kernel(own_ref, far_ref, check_ref, window_ref, v_ref, keep_ref, send_ref, tail_ref, buf, sems):
    for step in range(STEPS):
        block_copy(window_ref, buf, sems, step).start()
    core = lax.axis_index("core")
    pcol = (lax.axis_index("x") * 4 + lax.axis_index("zl")) * 2 + core
    lead = flag(lax.axis_index("y") % 2)
    top = flag(lax.axis_index("y") // 2)
    own, far = (interleaved(lead, ref[0], ref[1]) for ref in (own_ref, far_ref))
    block = jnp.concatenate([jnp.where(top > 0.5, own, far), jnp.where(top > 0.5, far, own)], axis=0)
    block = unit_lower(block, pcol * v_ref.shape[0])
    v_ref[...] = block
    right = right3(block, 0)
    line = lax.broadcasted_iota(jnp.int32, (8, check_ref.shape[1]), 0)
    tail = jnp.where(line == 0, check_ref[...], jnp.where(line == 1, 1.0, 0.0))
    half, rows = STEPS // 2, window_ref.shape[0] // STEPS
    for step in range(STEPS):
        block_copy(window_ref, buf, sems, step).wait()
        chunk = buf[step * rows : (step + 1) * rows]
        if step == 0:
            chunk = jnp.concatenate([chunk, tail], axis=0)
        x = mm3(left3(chunk, 1), right, NN)
        if step == 0:
            tail_ref[...] = x[rows:]
            x = x[:rows]
        part = slice(step % half * rows, (step % half + 1) * rows)

        @pl.when(core == step // half)
        def _():
            keep_ref[part] = x

        @pl.when(core != step // half)
        def _():
            send_ref[part] = x


def cols_call(own, far, check, window):
    n_rows, n_cols = window.shape
    kdim = own.shape[3]
    half = near_f32(n_rows // 2, kdim)
    return pl.pallas_call(
        cols_kernel,
        in_specs=[VMEM, VMEM, VMEM, HBM],
        out_specs=[VMEM] * 4,
        out_shape=[near_f32(n_cols, kdim), half, half, near_f32(8, kdim)],
        scratch_shapes=staged((n_rows, n_cols)),
        name="cols",
    )(vmem(own), vmem(far), check.reshape(1, n_cols), window)


def prep_kernel(v_ref, u_ref, check_ref, turned_ref, part_ref):
    upper = right3(triu(u_ref), 1)
    rows = v_ref.shape[0] // STEPS
    total = None
    for step in range(STEPS):
        part = slice(step * rows, (step + 1) * rows)
        block = v_ref[part]
        turned_ref[part] = left3(mm3(left3(block, 1), upper, NT), 1)
        sums = mm(jnp.broadcast_to(check_ref[:, part], (8, rows)), block, NN)
        total = sums if step == 0 else total + sums
    part_ref[...] = total[:1]


def prep_call(v_rows, factor, check):
    n_rows, kdim = v_rows.shape
    return pl.pallas_call(
        prep_kernel,
        in_specs=[VMEM] * 3,
        out_specs=[VMEM] * 2,
        out_shape=[jax.ShapeDtypeStruct((n_rows, 3 * kdim), jnp.bfloat16), far_f32(1, kdim)],
        name="prep",
    )(v_rows, factor, check.reshape(1, n_rows))


def slice_kernel(own_ref, far_ref, w_ref, c_ref, u_ref, part_ref, g_ref, vec_ref):
    k_rows, n_cols = w_ref.shape
    kdim = u_ref.shape[0]
    small = own_ref[...] + far_ref[...]
    upper = triu(u_ref)
    scaled = small[k_rows + 1 : k_rows + 2] / math.sqrt(N)
    line = lax.broadcasted_iota(jnp.int32, (8, kdim), 0)
    turned = mm(jnp.broadcast_to(scaled, (8, kdim)), upper, NT)
    vec_ref[...] = jnp.where(line == 0, scaled, jnp.where(line == 1, small[k_rows : k_rows + 1], jnp.where(line == 2, turned, 0.0)))
    z = mm(small[:k_rows], upper, NN)
    g = w_ref[...] - mm(z, c_ref[...], NT)
    prow = lax.axis_index("y") * 4 + lax.axis_index("zh")
    owner = prow * k_rows + lax.broadcasted_iota(jnp.int32, (k_rows, kdim), 0)
    mine = lax.broadcasted_iota(jnp.int32, (k_rows, kdim), 1) == owner
    z_scaled = jnp.sum(z * scaled, axis=1, keepdims=True)
    partial = part_ref[...] - jnp.sum(jnp.where(mine, z_scaled, 0.0), axis=0, keepdims=True)
    row = lax.broadcasted_iota(jnp.int32, (k_rows, LANES), 0)
    extra = jnp.zeros((k_rows, LANES), jnp.float32)
    for i in range(kdim // LANES):
        extra = jnp.where(row == i, partial[:, i * LANES : (i + 1) * LANES], extra)
    for j in range(g_ref.shape[0]):
        g_ref[j, :, :n_cols] = g
        g_ref[j, :, n_cols:] = extra


def slice_call(own, far, w_slice, v_cols, factor, part):
    k_rows, n_cols = w_slice.shape
    kdim = factor.shape[0]
    return pl.pallas_call(
        slice_kernel,
        in_specs=[VMEM] * 6,
        out_specs=[VMEM] * 2,
        out_shape=[near_f32(4, k_rows, n_cols + LANES), near_f32(8, kdim)],
        name="slice",
    )(vmem(own), vmem(far), vmem(w_slice), vmem(v_cols), factor, part)


def left_kernel(own_ref, far_ref, c_ref, u_ref, vec_ref, row_ref, col_ref, window_ref, nrow_ref, ncol_ref, out_ref, buf, sems, done):
    for step in range(STEPS):
        block_copy(window_ref, buf, sems, step).start()
    right = right3(c_ref[...], 1)
    vec = vec_ref[...]
    turned = mm(vec, triu(u_ref), NN)
    ncol_ref[...] = col_ref[...] - mm3(left3(turned, 1), right, NT)[1:2]
    vec = left3(vec, 1)
    half, rows = STEPS // 2, window_ref.shape[0] // STEPS
    lead = flag(lax.axis_index("core"))
    for step in range(STEPS):
        piece = slice(step % half * rows, (step % half + 1) * rows)
        mine = lead if step < half else 1.0 - lead
        block = jnp.where(mine > 0.5, own_ref[piece], far_ref[piece])
        part = slice(step * rows, (step + 1) * rows)
        out = mm3(left3(block, 1), right, NT)
        block_copy(window_ref, buf, sems, step).wait()
        buf[part] = buf[part] - out
        block_copy(buf, out_ref, done, step).start()
        nrow_ref[:, part] = row_ref[:, part] - mm3(vec, right3(block, 1), NT)[:1]
    for step in range(STEPS):
        block_copy(buf, out_ref, done, step).wait()


def left_call(own, far, v_cols, factor, vectors, row_check, col_check, window):
    n_rows, n_cols = window.shape
    return pl.pallas_call(
        left_kernel,
        in_specs=[VMEM] * 7 + [HBM],
        out_specs=[VMEM, VMEM, HBM],
        out_shape=[near_f32(1, n_rows), near_f32(1, n_cols), far_f32(n_rows, n_cols)],
        scratch_shapes=staged((n_rows, n_cols)) + [pltpu.SemaphoreType.DMA((STEPS,))],
        name="left",
    )(
        vmem(own),
        vmem(far),
        vmem(v_cols),
        factor,
        vmem(vectors),
        row_check.reshape(1, n_rows),
        col_check.reshape(1, n_cols),
        window,
    )


def right_kernel(g_ref, vec_ref, row_ref, col_ref, turned_ref, window_ref, nrow_ref, ncol_ref, out_ref, tbuf, tsems, buf, sems, done):
    for step in range(STEPS):
        block_copy(turned_ref, tbuf, tsems, step).start()
        block_copy(window_ref, buf, sems, step).start()
    n_cols = window_ref.shape[1]
    kdim = g_ref.shape[0]
    g_all = g_ref[...]
    extra = jnp.sum(g_all[:, n_cols:].reshape(16, kdim // 16, LANES), axis=0)
    inner = jnp.concatenate([extra[i : i + 1] for i in range(kdim // LANES)], axis=1)
    inner = jnp.broadcast_to(inner, (LANES, kdim)).T
    right = right3(jnp.concatenate([g_all[:, :n_cols], inner], axis=1), 0)
    rows = window_ref.shape[0] // STEPS
    for step in range(STEPS):
        part = slice(step * rows, (step + 1) * rows)
        block_copy(turned_ref, tbuf, tsems, step).wait()
        left = tbuf[part]
        if step == 0:
            left = jnp.concatenate([left, left3(vec_ref[...], 1)], axis=0)
        out = mm3(left, right, NN)
        if step == 0:
            ncol_ref[...] = col_ref[...] - out[rows + 2 : rows + 3, :n_cols]
            out = out[:rows]
        block_copy(window_ref, buf, sems, step).wait()
        buf[part] = buf[part] - out[:, :n_cols]
        block_copy(buf, out_ref, done, step).start()
        nrow_ref[:, part] = row_ref[:, part] - out[:, n_cols:].T[:1]
    for step in range(STEPS):
        block_copy(buf, out_ref, done, step).wait()


def right_call(g_all, vectors, row_part, col_part, turned, window):
    n_rows, n_cols = window.shape
    return pl.pallas_call(
        right_kernel,
        in_specs=[VMEM] * 4 + [HBM] * 2,
        out_specs=[VMEM, VMEM, HBM],
        out_shape=[far_f32(1, n_rows), far_f32(1, n_cols), far_f32(n_rows, n_cols)],
        scratch_shapes=staged(turned.shape, turned.dtype) + staged((n_rows, n_cols)) + [pltpu.SemaphoreType.DMA((STEPS,))],
        name="right",
    )(vmem(g_all), vmem(vectors), vmem(row_part), vmem(col_part), turned, window)


def on_device(window, panel, factor, col_check, row_check):
    kdim = panel.shape[1]
    shard = panel.shape[0]
    n_rows, n_cols = window.shape

    line = gather(panel, "zl", 4)
    moved = lax.ppermute(line, AXES, transposition())
    mine = gather(line, "x", 4)
    other = swap(mine, "core", 2, 1)
    v_rows, w_part = rows_call(mine.reshape(-1, shard, kdim), other.reshape(-1, shard, kdim), window)
    w_part = reduce_scatter(w_part, "y", 4)
    near = swap(moved, "y", 4, 1)
    pair = jnp.stack([moved, near]).reshape(2, -1, shard, kdim)
    far = swap(pair, "y", 4, 2)
    w_slice = reduce_scatter(w_part, "zh", 4)

    v_cols, keep, send, tail = cols_call(pair, far, col_check, window)
    x_part = keep + swap(send, "core", 2, 1)
    small = jnp.concatenate([dot(w_slice, v_cols), tail], axis=0)
    x_part, small = reduce_both(x_part, small, "x", 4)
    both = jnp.concatenate([x_part, small], axis=0)
    total = jnp.sum(gather(both, "zl", 4).reshape((4,) + both.shape), axis=0)
    turned, row_part = prep_call(v_rows, factor, row_check)
    tall = x_part.shape[0]
    small = total[tall:]
    y_rows = gather(dot(total[:tall], jnp.triu(factor)), "x", 4)
    y_far = swap(y_rows, "core", 2, 1)
    small_far = swap(small, "core", 2, 1)
    g_parts, vectors = slice_call(small, small_far, w_slice, v_cols, factor, row_part)
    g_some = exchange(g_parts, "zh").reshape(-1, n_cols + LANES)
    g_all = gather(g_some, "y", 4)

    new_row, new_col, partly = left_call(y_rows, y_far, v_cols, factor, vectors, row_check, col_check, window)
    new_row, new_col, new_window = right_call(g_all, vectors, new_row, new_col, turned, partly)
    return new_window, new_col.reshape(n_cols), new_row.reshape(n_rows)


def solution(mesh):
    fine = Mesh(mesh.devices.reshape(SIZES), AXES)
    rows, cols = ("y", "zh"), ("x", "zl", "core")
    placed = (P(rows, cols), P(AXES, None), P(), P(cols), P(rows))
    return jax.shard_map(
        on_device,
        mesh=fine,
        in_specs=placed,
        out_specs=(P(rows, cols), P(cols), P(rows)),
        check_vma=False,
    )
```

```python
import math

import jax
import jax.numpy as jnp
from jax import lax
from jax.experimental import pallas as pl
from jax.experimental.pallas import tpu as pltpu
from jax.sharding import Mesh, PartitionSpec as P


N = 16384
AXES = ("y", "zh", "x", "zl", "core")
SIZES = (4, 4, 4, 4, 2)
PREC = lax.Precision.HIGH


def dot(left, right, dims=((1,), (0,))):
    return lax.dot_general(left, right, (dims, ((), ())), precision=PREC)


def unit_lower(values, row_start):
    rows = row_start + lax.broadcasted_iota(jnp.int32, values.shape, 0)
    cols = lax.broadcasted_iota(jnp.int32, values.shape, 1)
    return jnp.where(rows > cols, values, jnp.where(rows == cols, 1.0, 0.0))


def exchange(parts, axis):
    return lax.all_to_all(parts, axis, 0, 0)


def gather(block, axis, size):
    parts = exchange(jnp.broadcast_to(block[None], (size,) + block.shape), axis)
    return parts.reshape((size * block.shape[0],) + block.shape[1:])


def reduce_scatter(block, axis, size):
    rows = block.shape[0] // size
    return jnp.sum(exchange(block.reshape(size, rows, block.shape[1]), axis), axis=0)


def reduce_both(block, small, axis, size):
    rows = block.shape[0] // size
    cut = block.reshape(size, rows, block.shape[1])
    both = jnp.concatenate([cut, jnp.broadcast_to(small[None], (size,) + small.shape)], axis=1)
    total = jnp.sum(exchange(both, axis), axis=0)
    return total[:rows], total[rows:]


def swap(block, axis, size, bit):
    return lax.ppermute(block, axis, [(i, i ^ bit) for i in range(size)])


def transposition():
    pairs = []
    for y in range(4):
        for zh in range(4):
            for x in range(4):
                for zl in range(4):
                    for core in range(2):
                        src = (((y * 4 + zh) * 4 + x) * 4 + zl) * 2 + core
                        new_y = x % 2 * 2 + core
                        dst = (((new_y * 4 + zl) * 4 + y) * 4 + zh) * 2 + x // 2
                        pairs.append((src, dst))
    return pairs


def split(value):
    high = value.astype(jnp.bfloat16)
    return high, (value - high.astype(jnp.float32)).astype(jnp.bfloat16)


def left3(value, axis):
    high, low = split(value)
    return jnp.concatenate([high, high, low], axis=axis)


def right3(value, axis):
    high, low = split(value)
    return jnp.concatenate([high, low, high], axis=axis)


def mm3(left, right, dims):
    return lax.dot_general(left, right, (dims, ((), ())), preferred_element_type=jnp.float32)


def mm(left, right, dims):
    return mm3(left3(left, dims[0][0]), right3(right, dims[1][0]), dims)


def triu(ref):
    rows = lax.broadcasted_iota(jnp.int32, ref.shape, 0)
    cols = lax.broadcasted_iota(jnp.int32, ref.shape, 1)
    return jnp.where(rows <= cols, ref[...], 0.0)


NN = ((1,), (0,))
NT = ((1,), (1,))
TN = ((0,), (0,))
STEPS = 4
LANES = 128
VMEM = pl.BlockSpec(memory_space=pltpu.VMEM)
HBM = pl.BlockSpec(memory_space=pltpu.HBM)


def near_f32(*shape):
    return pltpu.VMEM(shape, jnp.float32)


def far_f32(*shape):
    return jax.ShapeDtypeStruct(shape, jnp.float32)


def vmem(value):
    return pltpu.with_memory_space_constraint(value, pltpu.VMEM)


def staged(shape, dtype=jnp.float32):
    return [pltpu.VMEM(shape, dtype), pltpu.SemaphoreType.DMA((STEPS,))]


def block_copy(src, dst, sems, step):
    rows = src.shape[0] // STEPS
    part = pl.ds(step * rows, rows)
    return pltpu.make_async_copy(src.at[part], dst.at[part], sems.at[step])


def interleaved(lead, own, far):
    groups, shard, kdim = own.shape
    first = jnp.where(lead > 0.5, own, far)
    second = jnp.where(lead > 0.5, far, own)
    return jnp.concatenate([first, second], axis=1).reshape(2 * groups * shard, kdim)


def flag(index):
    return jnp.where(index == 0, 1.0, 0.0)


def rows_kernel(mine_ref, other_ref, window_ref, v_ref, w_ref, buf, sems):
    for step in range(STEPS):
        block_copy(window_ref, buf, sems, step).start()
    lead = flag(lax.axis_index("core"))
    start = (lax.axis_index("y") * 4 + lax.axis_index("zh")) * v_ref.shape[0]
    groups, rows = mine_ref.shape[0] // STEPS, v_ref.shape[0] // STEPS
    for step in range(STEPS):
        mine, other = (ref[step * groups : (step + 1) * groups] for ref in (mine_ref, other_ref))
        block = unit_lower(interleaved(lead, mine, other), start + step * rows)
        part = slice(step * rows, (step + 1) * rows)
        v_ref[part] = block
        block_copy(window_ref, buf, sems, step).wait()
        w_part = mm(block, buf[part], TN)
        if step == 0:
            w_ref[...] = w_part
        else:
            w_ref[...] += w_part


def rows_call(mine, other, window):
    n_rows, n_cols = window.shape
    kdim = mine.shape[2]
    return pl.pallas_call(
        rows_kernel,
        in_specs=[VMEM, VMEM, HBM],
        out_specs=[VMEM] * 2,
        out_shape=[near_f32(n_rows, kdim), near_f32(kdim, n_cols)],
        scratch_shapes=staged((n_rows, n_cols)),
        name="rows",
    )(vmem(mine), vmem(other), window)


def cols_kernel(own_ref, far_ref, check_ref, window_ref, v_ref, keep_ref, send_ref, tail_ref, buf, sems):
    for step in range(STEPS):
        block_copy(window_ref, buf, sems, step).start()
    core = lax.axis_index("core")
    pcol = (lax.axis_index("x") * 4 + lax.axis_index("zl")) * 2 + core
    lead = flag(lax.axis_index("y") % 2)
    top = flag(lax.axis_index("y") // 2)
    own, far = (interleaved(lead, ref[0], ref[1]) for ref in (own_ref, far_ref))
    block = jnp.concatenate([jnp.where(top > 0.5, own, far), jnp.where(top > 0.5, far, own)], axis=0)
    block = unit_lower(block, pcol * v_ref.shape[0])
    v_ref[...] = block
    right = right3(block, 0)
    line = lax.broadcasted_iota(jnp.int32, (8, check_ref.shape[1]), 0)
    tail = jnp.where(line == 0, check_ref[...], jnp.where(line == 1, 1.0, 0.0))
    half, rows = STEPS // 2, window_ref.shape[0] // STEPS
    for step in range(STEPS):
        block_copy(window_ref, buf, sems, step).wait()
        chunk = buf[step * rows : (step + 1) * rows]
        if step == 0:
            chunk = jnp.concatenate([chunk, tail], axis=0)
        x = mm3(left3(chunk, 1), right, NN)
        if step == 0:
            tail_ref[...] = x[rows:]
            x = x[:rows]
        part = slice(step % half * rows, (step % half + 1) * rows)

        @pl.when(core == step // half)
        def _():
            keep_ref[part] = x

        @pl.when(core != step // half)
        def _():
            send_ref[part] = x


def cols_call(own, far, check, window):
    n_rows, n_cols = window.shape
    kdim = own.shape[3]
    half = near_f32(n_rows // 2, kdim)
    return pl.pallas_call(
        cols_kernel,
        in_specs=[VMEM, VMEM, VMEM, HBM],
        out_specs=[VMEM] * 4,
        out_shape=[near_f32(n_cols, kdim), half, half, near_f32(8, kdim)],
        scratch_shapes=staged((n_rows, n_cols)),
        name="cols",
    )(vmem(own), vmem(far), check.reshape(1, n_cols), window)


def prep_kernel(v_ref, u_ref, check_ref, turned_ref, part_ref, upper_ref):
    upper_ref[...] = triu(u_ref)
    upper = right3(upper_ref[...], 1)
    rows = v_ref.shape[0] // STEPS
    total = None
    for step in range(STEPS):
        part = slice(step * rows, (step + 1) * rows)
        block = v_ref[part]
        turned_ref[part] = left3(mm3(left3(block, 1), upper, NT), 1)
        sums = mm(jnp.broadcast_to(check_ref[:, part], (8, rows)), block, NN)
        total = sums if step == 0 else total + sums
    part_ref[...] = total[:1]


def prep_call(v_rows, factor, check):
    n_rows, kdim = v_rows.shape
    return pl.pallas_call(
        prep_kernel,
        in_specs=[VMEM] * 3,
        out_specs=[VMEM] * 3,
        out_shape=[jax.ShapeDtypeStruct((n_rows, 3 * kdim), jnp.bfloat16), near_f32(1, kdim), near_f32(kdim, kdim)],
        name="prep",
    )(v_rows, factor, check.reshape(1, n_rows))


def slice_kernel(own_ref, far_ref, w_ref, c_ref, u_ref, part_ref, g_ref, vec_ref):
    k_rows, n_cols = w_ref.shape
    kdim = u_ref.shape[0]
    small = own_ref[...] + far_ref[...]
    upper = u_ref[...]
    scaled = small[k_rows + 1 : k_rows + 2] / math.sqrt(N)
    line = lax.broadcasted_iota(jnp.int32, (8, kdim), 0)
    turned = mm(jnp.broadcast_to(scaled, (8, kdim)), upper, NT)
    vec_ref[...] = jnp.where(line == 0, scaled, jnp.where(line == 1, small[k_rows : k_rows + 1], jnp.where(line == 2, turned, 0.0)))
    z = mm(small[:k_rows], upper, NN)
    g = w_ref[...] - mm(z, c_ref[...], NT)
    prow = lax.axis_index("y") * 4 + lax.axis_index("zh")
    owner = prow * k_rows + lax.broadcasted_iota(jnp.int32, (k_rows, kdim), 0)
    mine = lax.broadcasted_iota(jnp.int32, (k_rows, kdim), 1) == owner
    z_scaled = jnp.sum(z * scaled, axis=1, keepdims=True)
    partial = part_ref[...] - jnp.sum(jnp.where(mine, z_scaled, 0.0), axis=0, keepdims=True)
    row = lax.broadcasted_iota(jnp.int32, (k_rows, LANES), 0)
    extra = jnp.zeros((k_rows, LANES), jnp.float32)
    for i in range(kdim // LANES):
        extra = jnp.where(row == i, partial[:, i * LANES : (i + 1) * LANES], extra)
    for j in range(g_ref.shape[0]):
        g_ref[j, :, :n_cols] = g
        g_ref[j, :, n_cols:] = extra


def slice_call(own, far, w_slice, v_cols, factor, part):
    k_rows, n_cols = w_slice.shape
    kdim = factor.shape[0]
    return pl.pallas_call(
        slice_kernel,
        in_specs=[VMEM] * 6,
        out_specs=[VMEM] * 2,
        out_shape=[near_f32(4, k_rows, n_cols + LANES), near_f32(8, kdim)],
        name="slice",
    )(vmem(own), vmem(far), vmem(w_slice), vmem(v_cols), vmem(factor), vmem(part))


def left_kernel(own_ref, far_ref, c_ref, u_ref, vec_ref, row_ref, col_ref, window_ref, nrow_ref, ncol_ref, out_ref, buf, sems, done):
    for step in range(STEPS):
        block_copy(window_ref, buf, sems, step).start()
    right = right3(c_ref[...], 1)
    vec = vec_ref[...]
    turned = mm(vec, u_ref[...], NN)
    ncol_ref[...] = col_ref[...] - mm3(left3(turned, 1), right, NT)[1:2]
    vec = left3(vec, 1)
    half, rows = STEPS // 2, window_ref.shape[0] // STEPS
    lead = flag(lax.axis_index("core"))
    for step in range(STEPS):
        piece = slice(step % half * rows, (step % half + 1) * rows)
        mine = lead if step < half else 1.0 - lead
        block = jnp.where(mine > 0.5, own_ref[piece], far_ref[piece])
        part = slice(step * rows, (step + 1) * rows)
        out = mm3(left3(block, 1), right, NT)
        block_copy(window_ref, buf, sems, step).wait()
        buf[part] = buf[part] - out
        block_copy(buf, out_ref, done, step).start()
        nrow_ref[:, part] = row_ref[:, part] - mm3(vec, right3(block, 1), NT)[:1]
    for step in range(STEPS):
        block_copy(buf, out_ref, done, step).wait()


def left_call(own, far, v_cols, factor, vectors, row_check, col_check, window):
    n_rows, n_cols = window.shape
    return pl.pallas_call(
        left_kernel,
        in_specs=[VMEM] * 7 + [HBM],
        out_specs=[VMEM, VMEM, HBM],
        out_shape=[near_f32(1, n_rows), near_f32(1, n_cols), far_f32(n_rows, n_cols)],
        scratch_shapes=staged((n_rows, n_cols)) + [pltpu.SemaphoreType.DMA((STEPS,))],
        name="left",
    )(
        own,
        vmem(far),
        vmem(v_cols),
        vmem(factor),
        vmem(vectors),
        row_check.reshape(1, n_rows),
        col_check.reshape(1, n_cols),
        window,
    )


def right_kernel(g_ref, vec_ref, row_ref, col_ref, turned_ref, window_ref, nrow_ref, ncol_ref, out_ref, tbuf, tsems, buf, sems, done):
    for step in range(STEPS):
        block_copy(turned_ref, tbuf, tsems, step).start()
        block_copy(window_ref, buf, sems, step).start()
    n_cols = window_ref.shape[1]
    kdim = g_ref.shape[0]
    g_all = g_ref[...]
    extra = jnp.sum(g_all[:, n_cols:].reshape(16, kdim // 16, LANES), axis=0)
    inner = jnp.concatenate([extra[i : i + 1] for i in range(kdim // LANES)], axis=1)
    inner = jnp.broadcast_to(inner, (LANES, kdim)).T
    right = right3(jnp.concatenate([g_all[:, :n_cols], inner], axis=1), 0)
    rows = window_ref.shape[0] // STEPS
    for step in range(STEPS):
        part = slice(step * rows, (step + 1) * rows)
        block_copy(turned_ref, tbuf, tsems, step).wait()
        left = tbuf[part]
        if step == 0:
            left = jnp.concatenate([left, left3(vec_ref[...], 1)], axis=0)
        out = mm3(left, right, NN)
        if step == 0:
            ncol_ref[...] = col_ref[...] - out[rows + 2 : rows + 3, :n_cols]
            out = out[:rows]
        block_copy(window_ref, buf, sems, step).wait()
        buf[part] = buf[part] - out[:, :n_cols]
        block_copy(buf, out_ref, done, step).start()
        nrow_ref[:, part] = row_ref[:, part] - out[:, n_cols:].T[:1]
    for step in range(STEPS):
        block_copy(buf, out_ref, done, step).wait()


def right_call(g_all, vectors, row_part, col_part, turned, window):
    n_rows, n_cols = window.shape
    return pl.pallas_call(
        right_kernel,
        in_specs=[VMEM] * 4 + [HBM] * 2,
        out_specs=[VMEM, VMEM, HBM],
        out_shape=[far_f32(1, n_rows), far_f32(1, n_cols), far_f32(n_rows, n_cols)],
        scratch_shapes=staged(turned.shape, turned.dtype) + staged((n_rows, n_cols)) + [pltpu.SemaphoreType.DMA((STEPS,))],
        name="right",
    )(vmem(g_all), vmem(vectors), vmem(row_part), vmem(col_part), turned, window)


def on_device(window, panel, factor, col_check, row_check):
    kdim = panel.shape[1]
    shard = panel.shape[0]
    n_rows, n_cols = window.shape

    line = gather(panel, "zl", 4)
    moved = lax.ppermute(line, AXES, transposition())
    mine = gather(line, "x", 4)
    other = swap(mine, "core", 2, 1)
    v_rows, w_part = rows_call(mine.reshape(-1, shard, kdim), other.reshape(-1, shard, kdim), window)
    w_part = reduce_scatter(w_part, "y", 4)
    near = swap(moved, "y", 4, 1)
    pair = jnp.stack([moved, near]).reshape(2, -1, shard, kdim)
    far = swap(pair, "y", 4, 2)
    w_slice = reduce_scatter(w_part, "zh", 4)

    v_cols, keep, send, tail = cols_call(pair, far, col_check, window)
    x_part = keep + swap(send, "core", 2, 1)
    small = jnp.concatenate([dot(w_slice, v_cols), tail], axis=0)
    x_part, small = reduce_both(x_part, small, "x", 4)
    both = jnp.concatenate([x_part, small], axis=0)
    total = jnp.sum(gather(both, "zl", 4).reshape((4,) + both.shape), axis=0)
    turned, row_part, upper = prep_call(v_rows, factor, row_check)
    tall = x_part.shape[0]
    small = total[tall:]
    y_rows = gather(dot(total[:tall], upper), "x", 4)
    y_far = swap(y_rows, "core", 2, 1)
    small_far = swap(small, "core", 2, 1)
    g_parts, vectors = slice_call(small, small_far, w_slice, v_cols, upper, row_part)
    g_some = exchange(g_parts, "zh").reshape(-1, n_cols + LANES)
    g_all = gather(g_some, "y", 4)

    new_row, new_col, partly = left_call(y_rows, y_far, v_cols, upper, vectors, row_check, col_check, window)
    new_row, new_col, new_window = right_call(g_all, vectors, new_row, new_col, turned, partly)
    return new_window, new_col.reshape(n_cols), new_row.reshape(n_rows)


def solution(mesh):
    fine = Mesh(mesh.devices.reshape(SIZES), AXES)
    rows, cols = ("y", "zh"), ("x", "zl", "core")
    placed = (P(rows, cols), P(AXES, None), P(), P(cols), P(rows))
    return jax.shard_map(
        on_device,
        mesh=fine,
        in_specs=placed,
        out_specs=(P(rows, cols), P(cols), P(rows)),
        check_vma=False,
    )
```
